32 devices in a mesh: groups: 2 (over y), chan: 4 (over z), tm: 2 (over core), dp: 2 (over x).
Axes of the slice: x: 2, y: 2, z: 4, core: 2. Of those that a mesh axis runs over, the one named last changes fastest.
Arguments:
- features: bfloat16 [384, 4, 8, 256], P('chan', ('groups', 'dp'), 'tm'), parts along dimension 1, may hold values from -6 to 6
- kernel: bfloat16 [384, 27, 384], P('chan'), may hold values from -0.078125 to 0.078125
- cotangent: bfloat16 [384, 4, 8, 256], P('chan', ('groups', 'dp'), 'tm'), parts along dimension 1, may hold values from -6 to 6
Outputs:
- conv_out: bfloat16 [384, 4, 8, 256], P('chan', ('groups', 'dp'), 'tm'), parts along dimension 1
- feature_grad: bfloat16 [384, 4, 8, 256], P('chan', ('groups', 'dp'), 'tm'), parts along dimension 1
- kernel_grad: float32 [768, 27, 384], P(('groups', 'chan')), parts along dimension 0
The draws below stay inside these ranges and needn't reach their ends.
There are 2 independent parts, one for each index of `groups`. The reference program is written for one: setup_inputs(seed, part) draws one part's arguments, and reference() takes and returns one part's arrays. A program takes and returns all parts, laid end to end along the dimension named above; an argument that names none is the same for every part. Nothing has to cross between parts.
All inputs are finite; a program needn't handle non-finite values.
Results may differ from the reference program's by a relative error of at most 0.0051.
Values may be sent and summed in bfloat16 or wider, within the bound.
A program may use at most 128 MiB of HBM per device.

```python
import math
import jax
import jax.numpy as jnp
from jax import lax

C = 384
H_ROWS = 4
WID = 64
CLIPS = 2
FRAMES = 8
PIXELS = 256


def with_spikes(entries, stream_key, source, target, shards_of, factor):
    def block_of(axis_at):
        return (jnp.arange(entries.shape[axis_at]) // (entries.shape[axis_at] // shards_of)).reshape((-1,) + (1,) * (entries.ndim - 1 - axis_at))

    first = jax.random.permutation(stream_key, shards_of)[block_of(target)]
    far = (block_of(target) + shards_of // 2) % shards_of
    return jnp.where((block_of(source) == first) | (block_of(source) == far), factor * entries, entries)


def block_levels(key, extent, shards, least, high):
    gain, own = 1.0, jax.random.fold_in(key, 6)
    for position, shards_of in shards:
        draws = jnp.exp(jax.random.uniform(jax.random.fold_in(own, position), (shards_of,), jnp.float32, least / len(shards), high / len(shards)))
        gain = gain * jnp.repeat(draws, extent[position] // shards_of).reshape([-1 if axis == position else 1 for axis in range(len(extent))])
    return gain


def gaussian(stream_key, shape, scale, limit, pieces=(), kind=jnp.bfloat16):
    loudness = block_levels(stream_key, shape, pieces, -0.22, 0.18) if pieces else 1.0
    drawn = jax.random.normal(stream_key, shape, jnp.float32) * scale * loudness
    return jnp.minimum(jnp.maximum(drawn, -limit), limit).astype(kind)


def gaussian_with(rng, extent, scale, reach, shards, heavy, kind=jnp.bfloat16):
    array = scale * jax.random.normal(rng, extent, jnp.float32)
    if shards:
        array = array * block_levels(rng, extent, shards, -0.22, 0.18)
    return jnp.clip(with_spikes(array, jax.random.fold_in(rng, 3), *heavy), -reach, reach).astype(kind)


def setup_inputs(seed: int = 0, part: int = 0) -> dict:
    streams_of = jax.random.split(jax.random.key(seed), 4)
    part_keys = jax.random.split(jax.random.fold_in(streams_of[3], part), 4)
    features = gaussian(part_keys[0], (C, CLIPS, FRAMES, PIXELS), 1.0, 6.0, ((0, 4), (1, 2), (2, 2)))
    kernel = gaussian_with(streams_of[1], (C, 27, C), (27 * C) ** -0.5, 0.078125, ((0, 4),), (0, 2, 4, 2.0))
    cotangent = gaussian(part_keys[2], (C, CLIPS, FRAMES, PIXELS), 1.0, 6.0, ((0, 4), (1, 2), (2, 2)))
    return {"features": features, "kernel": kernel, "cotangent": cotangent}


def reference(features, kernel, cotangent):
    widened = features.astype(jnp.float32)
    logistic = jax.nn.sigmoid(widened)
    activation = lax.optimization_barrier((widened * logistic).astype(jnp.bfloat16)).astype(jnp.float32)
    slope_factor = logistic * (1.0 + widened * (1.0 - logistic))
    grid_shape = (C, CLIPS, FRAMES, H_ROWS, WID)
    activation_grid = jnp.pad(activation.reshape(grid_shape), ((0, 0), (0, 0), (2, 0), (1, 1), (1, 1)))
    cotangent_wide = cotangent.astype(jnp.float32)
    cotangent_grid = jnp.pad(cotangent_wide.reshape(grid_shape), ((0, 0), (0, 0), (0, 2), (1, 1), (1, 1)))
    cotangent_rows = cotangent_wide.reshape(C, -1)
    kernel_wide = kernel.astype(jnp.float32)
    out_sum = jnp.zeros((C, CLIPS * FRAMES * PIXELS), jnp.float32)
    before_slope = jnp.zeros((C, CLIPS * FRAMES * PIXELS), jnp.float32)
    grad_parts = []
    for temporal in range(3):
        for vertical in range(3):
            for horizontal in range(3):
                tap_index = 9 * temporal + 3 * vertical + horizontal
                tap_matrix = kernel_wide[:, tap_index, :]
                shifted = activation_grid[:, :, temporal:temporal + FRAMES, vertical:vertical + H_ROWS, horizontal:horizontal + WID].reshape(C, -1)
                out_sum = out_sum + jnp.dot(tap_matrix, shifted, preferred_element_type=jnp.float32)
                grad_parts.append(jnp.dot(cotangent_rows, shifted.T, preferred_element_type=jnp.float32))
                flipped = cotangent_grid[:, :, 2 - temporal:2 - temporal + FRAMES, 2 - vertical:2 - vertical + H_ROWS, 2 - horizontal:2 - horizontal + WID].reshape(C, -1)
                before_slope = before_slope + jnp.dot(tap_matrix.T, flipped, preferred_element_type=jnp.float32)
    grad_scale = 1.0 / math.sqrt(CLIPS * FRAMES * PIXELS)
    conv_out = out_sum.reshape(features.shape).astype(jnp.bfloat16)
    feature_grad = (before_slope.reshape(features.shape) * slope_factor).astype(jnp.bfloat16)
    kernel_grad = jnp.stack(grad_parts, axis=1) * grad_scale
    return (conv_out, feature_grad, kernel_grad)
```

```python
import functools
import math

import jax
import jax.numpy as jnp
from jax import lax
from jax.experimental import pallas as pl
from jax.experimental.pallas import tpu as pltpu
from jax.sharding import PartitionSpec as P

WID = 64


def from_behind(x, axis, by):
    size = lax.axis_size(axis)
    pairs = [(i, i + by) for i in range(size) if 0 <= i + by < size]
    return lax.ppermute(x, axis, pairs)


def padded_copies(block):
    pixels = block.shape[-1]
    column = lax.broadcasted_iota(jnp.int32, (pixels,), 0) % WID
    nothing = jnp.zeros((), block.dtype)
    widths = [(0, 0), (0, 0), (0, 0), (WID + 1, WID + 1)]
    left_cut = jnp.pad(jnp.where(column == WID - 1, nothing, block), widths)
    untouched = jnp.pad(block, widths)
    right_cut = jnp.pad(jnp.where(column == 0, nothing, block), widths)
    return (left_cut, untouched, right_cut)


def tap_window(copies, first_frame, vertical, horizontal, frames, pixels):
    source = copies[horizontal]
    offset = vertical * WID + horizontal
    return source[:, :, first_frame : first_frame + frames, offset : offset + pixels]


def stacked_taps(copies, first_frame, flipped, frames, pixels):
    pieces = []
    for vertical in range(3):
        for horizontal in range(3):
            if flipped:
                pieces.append(
                    tap_window(copies, first_frame, 2 - vertical, 2 - horizontal, frames, pixels)
                )
            else:
                pieces.append(tap_window(copies, first_frame, vertical, horizontal, frames, pixels))
    concatenated = jnp.concatenate(pieces, axis=0)
    return concatenated.reshape(concatenated.shape[0], -1)


def local(features, kernel, cotangent):
    channels, clip_count, frames, pixels = features.shape
    flat_length = clip_count * frames * pixels
    widened = features.astype(jnp.float32)
    logistic = jax.nn.sigmoid(widened)
    activation = (widened * logistic).astype(jnp.bfloat16)
    slope_factor = logistic * (1.0 + widened * (1.0 - logistic))
    earlier = from_behind(activation[:, :, frames - 2 :, :], "tm", 1)
    extended = jnp.concatenate([earlier, activation], axis=2)
    upcoming = from_behind(cotangent[:, :, :2, :], "tm", -1)
    later_padded = jnp.concatenate([cotangent, upcoming], axis=2)
    cotangent_rows = cotangent.reshape(channels, -1)
    portion = lax.all_gather(extended, "chan", axis=0, tiled=True)
    out_sum = jnp.zeros((channels, flat_length), jnp.float32)
    amount = portion.shape[0]
    copies = padded_copies(portion)
    kernel_cols = kernel
    grad_parts = []
    for forward_temporal in range(3):
        stacked = stacked_taps(copies, forward_temporal, False, frames, pixels)
        weights = kernel_cols[:, 9 * forward_temporal : 9 * forward_temporal + 9, :].reshape(
            channels, 9 * amount
        )
        out_sum = out_sum + jnp.dot(weights, stacked, preferred_element_type=jnp.float32)
        grad_parts.append(
            lax.dot_general(
                cotangent_rows,
                stacked,
                (((1,), (1,)), ((), ())),
                preferred_element_type=jnp.float32,
            ).reshape(channels, 9, amount)
        )
    grad_sum = jnp.concatenate(grad_parts, axis=1)
    out_sum, grad_sum = (out_sum, grad_sum)
    conv_out = out_sum.reshape(features.shape).astype(jnp.bfloat16)
    position_count = lax.axis_size("dp") * lax.axis_size("tm") * flat_length
    kernel_grad = lax.psum(grad_sum, ("tm", "dp")) * (1.0 / math.sqrt(position_count))
    padded_later = padded_copies(later_padded)
    later_stacks = [
        stacked_taps(padded_later, 2 - temporal, True, frames, pixels) for temporal in range(3)
    ]
    amount = channels * lax.axis_size("chan")
    kernel_cols = kernel
    summed = jnp.zeros((amount, flat_length), jnp.float32)
    for temporal in range(3):
        weights = jnp.transpose(
            kernel_cols[:, 9 * temporal : 9 * temporal + 9, :], (2, 1, 0)
        ).reshape(amount, 9 * channels)
        summed = summed + jnp.dot(
            weights, later_stacks[temporal], preferred_element_type=jnp.float32
        )
    before_slope = lax.psum_scatter(
        summed.reshape(amount, clip_count, frames, pixels), "chan", scatter_dimension=0, tiled=True
    )
    feature_grad = (before_slope * slope_factor).astype(jnp.bfloat16)
    return (conv_out, feature_grad, kernel_grad)


def moved(x, rows, columns, pixels):
    step = rows * WID + columns
    place = lax.broadcasted_iota(jnp.int32, x.shape, len(x.shape) - 1)
    row, column = place // WID + rows, place % WID + columns
    out = x if step == 0 else pltpu.roll(x, (-step) % pixels, len(x.shape) - 1)
    inside = None
    if rows:
        inside = (row >= 0) & (row < pixels // WID)
    if columns:
        within = (column >= 0) & (column < WID)
        inside = within if inside is None else inside & within
    return out if inside is None else jnp.where(inside, out, 0.0)


def silu(x):
    wide = x.astype(jnp.float32)
    return wide * jax.nn.sigmoid(wide)


def body(
    sizes,
    f_ref, w_hbm, g_ref,
    out_ref, fg_ref, mine_ref, theirs_ref,
    w_ref, stack, turned, act, cot_in, part, right_in, left_in, taps,
    w_sem, gather_right, gather_left, gather_recv, pair_send, pair_recv, own_send, own_recv,
    cot_send, cot_recv, halo_send, halo_recv, right_send, right_recv, left_send, left_recv,
    sum_send, sum_recv, keep_send, keep_recv, done_send, done_recv,
):
    n, lanes, rows = sizes
    frames, c, pixels = f_ref.shape
    full = c * n
    half = c // 2
    long = frames * pixels
    every = 2 * frames
    groups = full // lanes
    per = c // rows
    total_pieces = per * n
    z, t, d = lax.axis_index("chan"), lax.axis_index("tm"), lax.axis_index("dp")

    def remote(src, dst, send, recv, **where):
        return pltpu.make_async_remote_copy(
            src_ref=src, dst_ref=dst, send_sem=send, recv_sem=recv,
            device_id=where, device_id_type=pl.DeviceIdType.MESH,
        )

    weights = pltpu.make_async_copy(w_hbm, w_ref, w_sem)
    weights.start()
    barrier = pltpu.get_barrier_semaphore()

    def greet(**where):
        pl.semaphore_signal(barrier, inc=1, device_id=where, device_id_type=pl.DeviceIdType.MESH)

    greet(tm=1 - t)
    greet(dp=1 - d)

    @pl.when(z < n - 1)
    def _():
        greet(chan=z + 1)

    @pl.when(z > 0)
    def _():
        greet(chan=z - 1)

    def half_rows(which):
        return pl.ds(pl.multiple_of(which * half, half), half)

    def frame_lanes(s):
        return pl.ds(pl.multiple_of(s * pixels, pixels), pixels)

    def own_lanes(which):
        return pl.ds(pl.multiple_of((which * frames + 2) * pixels, pixels), long)

    def shard_rows(q):
        return pl.ds(pl.multiple_of(q * c, c), c)

    def piece(p, which):
        return act.at[pl.ds(pl.multiple_of(p * rows, rows), rows), own_lanes(which)]

    for s in range(frames):
        act[shard_rows(z), frame_lanes(t * frames + s + 2)] = silu(f_ref[s]).astype(jnp.bfloat16)

    def stack_frame(x, s, at):
        wide = x.astype(jnp.float32)
        for i in range(3):
            for j in range(3):
                stack[3 * i + j, at, frame_lanes(s)] = moved(wide, 1 - i, 1 - j, pixels).astype(jnp.bfloat16)

    everything = pl.ds(0, c)

    def own_frame(s, _):
        stack_frame(g_ref[s], t * frames + s, everything)
        return 0

    lax.fori_loop(0, frames, own_frame, 0)

    @pl.when((z > 0) & (z < n - 1))
    def _():
        pl.semaphore_wait(barrier, 4)

    @pl.when((z == 0) | (z == n - 1))
    def _():
        pl.semaphore_wait(barrier, 3)

    def pass_right(p):
        return remote(piece(p, t), piece(p, t), gather_right.at[p], gather_recv.at[p], chan=z + 1)

    def pass_left(p):
        return remote(piece(p, t), piece(p, t), gather_left.at[p], gather_recv.at[p], chan=z - 1)

    def pair_copy(p, which):
        return remote(piece(p, which), piece(p, which), pair_send.at[p], pair_recv.at[p], tm=1 - t)

    def own_copy(which):
        place = act.at[shard_rows(z), own_lanes(which)]
        return remote(place, place, own_send, own_recv, tm=1 - t)

    def cot_copy():
        return remote(
            g_ref.at[:, half_rows(1 - t)], cot_in.at[:, half_rows(1 - t)], cot_send, cot_recv, tm=1 - t
        )

    def halo_copy():
        return remote(
            g_ref.at[pl.ds(0, 2), half_rows(1)], cot_in.at[pl.ds(0, 2), half_rows(1)], halo_send, halo_recv, tm=1 - t
        )

    for k in range(per):
        @pl.when(z < n - 1)
        def _():
            pass_right(z * per + per - 1 - k).start()

        @pl.when(z > 0)
        def _():
            pass_left(z * per + k).start()

    cot_copy().start()

    @pl.when(t == 1)
    def _():
        halo_copy().start()

    own_copy(t).start()

    act[:, 0 : 2 * pixels] = jnp.zeros((full, 2 * pixels), jnp.bfloat16)
    stack[:, :, every * pixels : (every + 2) * pixels] = jnp.zeros((9, c, 2 * pixels), jnp.bfloat16)
    weights.wait()
    turned[...] = jnp.transpose(w_ref[...].reshape(27 * c, full))

    cot_copy().wait_recv()

    def other_frame(s, _):
        stack_frame(cot_in[s, half_rows(t), :], (1 - t) * frames + s, half_rows(t))
        return 0

    lax.fori_loop(0, frames, other_frame, 0)

    @pl.when(t == 0)
    def _():
        halo_copy().wait_recv()

        def next_frame(s, _):
            stack_frame(cot_in[s, half_rows(1), :], frames + s, half_rows(1))
            return 0

        lax.fori_loop(0, 2, next_frame, 0)

    def tick(k):
        @pl.when((z + 1) * per + k < total_pieces)
        def _():
            p = (z + 1) * per + k
            pass_left(p).wait_recv()

            @pl.when(z > 0)
            def _():
                pass_left(p).start()

            pair_copy(p, t).start()

        @pl.when(z * per - 1 - k >= 0)
        def _():
            p = z * per - 1 - k
            pass_right(p).wait_recv()

            @pl.when(z < n - 1)
            def _():
                pass_right(p).start()

            pair_copy(p, t).start()

    def pair_tick(k):
        @pl.when((z + 1) * per + k < total_pieces)
        def _():
            pair_copy((z + 1) * per + k, 1 - t).wait_recv()

        @pl.when(z * per - 1 - k >= 0)
        def _():
            pair_copy(z * per - 1 - k, 1 - t).wait_recv()

    def group(i):
        first, last = (z + 1) // 2, 2 - 2 * (z // 2)
        return (first, 3 - first - last, last)[i]

    def cell(ref, i, a, which):
        return ref.at[group(i), which, pl.ds(9 * a, 9)]

    def sum_copy(i, a):
        return remote(
            cell(mine_ref, i, a, t), cell(theirs_ref, i, a, t), sum_send.at[3 * i + a], sum_recv.at[3 * i + a], dp=1 - d
        )

    def keep_copy(i, a, which):
        place = cell(mine_ref, i, a, which)
        return remote(place, place, keep_send.at[3 * i + a], keep_recv.at[3 * i + a], tm=1 - t)

    def done_copy(i, a, which):
        place = cell(theirs_ref, i, a, which)
        return remote(place, place, done_send.at[3 * i + a], done_recv.at[3 * i + a], tm=1 - t)

    def kernel_terms(i):
        at = pl.ds(pl.multiple_of(group(i) * lanes, lanes), lanes)
        for a in range(3):
            held = stack[:, half_rows(t), (2 - a) * pixels : every * pixels].reshape(9 * half, (6 + a) * pixels)
            terms = lax.dot_general(
                held, act[at, 2 * pixels : (8 + a) * pixels], (((1,), (1,)), ((), ())),
                preferred_element_type=jnp.float32,
            )
            mine_ref[group(i), t, 9 * a : 9 * a + 9] = terms.reshape(9, half, lanes).astype(jnp.bfloat16)
            sum_copy(i, a).start()
            keep_copy(i, a, t).start()

    def before(s):
        rhs = jnp.concatenate(
            [stack[:, :, frame_lanes(t * frames + s + 2 - a)].reshape(9 * c, pixels) for a in range(3)], axis=0
        )
        total = jnp.dot(turned[...], rhs, preferred_element_type=jnp.float32)
        for q in range(n):
            part[q, s] = total[q * c : (q + 1) * c].astype(jnp.bfloat16)

    def share_right(q, src):
        return remote(src.at[q], right_in.at[q], right_send.at[q], right_recv.at[q], chan=z + 1)

    def share_left(q, src):
        return remote(src.at[q], left_in.at[q], left_send.at[q], left_recv.at[q], chan=z - 1)

    def add_part(held, q):
        for s in range(frames):
            held[q, s] = (held[q, s].astype(jnp.float32) + part[q, s].astype(jnp.float32)).astype(jnp.bfloat16)

    def first_shares():
        for j in range(n - 1):
            @pl.when(z == 0)
            def _():
                share_right(n - 1 - j, part).start()

            @pl.when(z == n - 1)
            def _():
                share_left(j, part).start()

    def wait_share(held, q, sem):
        remote(held.at[q], held.at[q], right_send.at[q], sem.at[q], chan=lax.rem(z + 1, n)).wait_recv()

    def relay_right(j, ahead):
        @pl.when((z > 0) & (z < n - 1 - j) & ahead)
        def _():
            wait_share(right_in, n - 1 - j, right_recv)
            add_part(right_in, n - 1 - j)
            share_right(n - 1 - j, right_in).start()

    def relay_left(j, ahead):
        @pl.when((z < n - 1) & (z > j) & ahead)
        def _():
            wait_share(left_in, j, left_recv)
            add_part(left_in, j)
            share_left(j, left_in).start()

    def relay(j):
        lower = 2 * z < n
        if j < n - 1:
            relay_right(j, lower)
            relay_left(j, jnp.logical_not(lower))
        if j > 0:
            relay_right(j - 1, jnp.logical_not(lower))
            relay_left(j - 1, lower)

    def convolve(u):
        rhs = jnp.concatenate([act[:, frame_lanes(t * frames + u + a)] for a in range(3)], axis=0)
        lhs = jnp.concatenate([w_ref[9 * a : 9 * a + 9].reshape(9 * c, full) for a in range(3)], axis=1)
        taps[...] = jnp.dot(lhs, rhs, preferred_element_type=jnp.float32).reshape(9, c, pixels)
        result = jnp.zeros((c, pixels), jnp.float32)
        for i in range(3):
            for j in range(3):
                result = result + moved(taps[3 * i + j], i - 1, j - 1, pixels)
        out_ref[u] = result.astype(jnp.bfloat16)

    def forward(i, a):
        sum_copy(i, a).wait_recv()
        done_copy(i, a, t).start()

    before(0)
    tick(0)
    before(1)
    tick(1)
    own_copy(1 - t).wait_recv()
    pair_tick(0)
    pair_tick(1)
    kernel_terms(0)
    tick(2)
    before(2)
    before(3)
    first_shares()
    tick(3)
    tick(4)
    for k in (2, 3, 4):
        pair_tick(k)
    kernel_terms(1)
    tick(5)
    tick(6)
    relay(0)
    tick(7)
    tick(8)
    for k in (5, 6, 7, 8):
        pair_tick(k)
    kernel_terms(2)
    for a in range(3):
        forward(0, a)
    convolve(0)
    relay(1)
    convolve(1)
    relay(2)
    convolve(2)
    for a in range(3):
        forward(1, a)
    convolve(3)

    @pl.when(z > 0)
    def _():
        wait_share(right_in, z, right_recv)

    @pl.when(z < n - 1)
    def _():
        wait_share(left_in, z, left_recv)

    def slope_frame(s, _):
        wide = f_ref[s].astype(jnp.float32)
        logistic = jax.nn.sigmoid(wide)
        slope = logistic * (1.0 + wide * (1.0 - logistic))

        def keep(total):
            fg_ref[s] = (total * slope).astype(jnp.bfloat16)

        own = part[z, s].astype(jnp.float32)

        @pl.when(z == 0)
        def _():
            keep(own + left_in[z, s].astype(jnp.float32))

        @pl.when(z == n - 1)
        def _():
            keep(own + right_in[z, s].astype(jnp.float32))

        @pl.when((z > 0) & (z < n - 1))
        def _():
            keep(own + (left_in[z, s].astype(jnp.float32) + right_in[z, s].astype(jnp.float32)))

        return 0

    lax.fori_loop(0, frames, slope_frame, 0)
    for a in range(3):
        forward(2, a)

    for p in range(total_pieces):
        @pl.when((z < n - 1) & (p < (z + 1) * per))
        def _():
            pass_right(p).wait_send()

        @pl.when((z > 0) & (p >= z * per))
        def _():
            pass_left(p).wait_send()

        @pl.when((p < z * per) | (p >= (z + 1) * per))
        def _():
            pair_copy(p, t).wait_send()

    for j in range(n - 1):
        @pl.when(z < n - 1 - j)
        def _():
            share_right(n - 1 - j, right_in).wait_send()

        @pl.when(z > j)
        def _():
            share_left(j, left_in).wait_send()

    own_copy(t).wait_send()
    cot_copy().wait_send()

    @pl.when(t == 1)
    def _():
        halo_copy().wait_send()

    for i in range(groups):
        for a in range(3):
            sum_copy(i, a).wait_send()
            keep_copy(i, a, t).wait_send()
            keep_copy(i, a, 1 - t).wait_recv()
            done_copy(i, a, t).wait_send()
            done_copy(i, a, 1 - t).wait_recv()


def finish(scale, mine_ref, theirs_ref, out_hbm, held, sems):
    groups, halves, taps, half, lanes = mine_ref.shape
    chunk = 3

    def copy(k):
        at = pl.ds(k * chunk, chunk)
        return pltpu.make_async_copy(held.at[at], out_hbm.at[at], sems.at[k])

    for k in range(taps // chunk):
        at = slice(k * chunk, (k + 1) * chunk)
        for h in range(halves):
            for g in range(groups):
                held[at, h * half : (h + 1) * half, g * lanes : (g + 1) * lanes] = (
                    mine_ref[g, h, at].astype(jnp.float32) + theirs_ref[g, h, at].astype(jnp.float32)
                ) * scale
        copy(k).start()
    for k in range(taps // chunk):
        copy(k).wait()


LANES = 128


def fits(mesh, features, kernel):
    c, clips, frames, pixels = features.shape
    return (
        mesh.shape["tm"] == 2
        and mesh.shape["chan"] == 4
        and mesh.shape["dp"] == 2
        and clips == 1
        and frames == 4
        and c * mesh.shape["chan"] == kernel.shape[2]
        and kernel.shape[2] == 3 * LANES
        and pixels % 128 == 0
        and pixels % WID == 0
        and kernel.size * 20 + features.size * 96 < 56 * 2**20
    )


def fused(mesh, features, kernel, cotangent):
    c, clips, frames, pixels = features.shape
    n = mesh.shape["chan"]
    full = c * n
    scale = 1.0 / math.sqrt(mesh.shape["dp"] * mesh.shape["tm"] * clips * frames * pixels)
    by_frame = lambda x: jnp.transpose(x.reshape(c, frames, pixels), (1, 0, 2))
    back = lambda x: jnp.transpose(x, (1, 0, 2)).reshape(c, clips, frames, pixels)
    vmem = pl.BlockSpec(memory_space=pltpu.VMEM)
    b16, f32 = jnp.bfloat16, jnp.float32
    dma = pltpu.SemaphoreType.DMA
    half = c // 2
    groups = full // LANES
    rows = math.gcd(c, LANES)
    pieces = full // rows
    sums = 3 * groups
    limit = 8 * 2**20 + kernel.size * 14 + features.size * 64
    shards = pltpu.VMEM((n, frames, c, pixels), b16)
    halves = jax.ShapeDtypeStruct((groups, 2, 27, half, LANES), b16)
    conv_out, feature_grad, mine, theirs = pl.pallas_call(
        functools.partial(body, (n, LANES, rows)),
        out_shape=(
            jax.ShapeDtypeStruct((frames, c, pixels), b16),
            jax.ShapeDtypeStruct((frames, c, pixels), b16),
            halves, halves,
        ),
        in_specs=[vmem, pl.BlockSpec(memory_space=pltpu.HBM), vmem],
        out_specs=(vmem,) * 4,
        scratch_shapes=[
            pltpu.VMEM((27, c, full), b16),
            pltpu.VMEM((9, c, (2 * frames + 2) * pixels), b16),
            pltpu.VMEM((full, 27 * c), b16),
            pltpu.VMEM((full, (2 * frames + 2) * pixels), b16),
            pltpu.VMEM((frames, c, pixels), b16),
            shards, shards, shards,
            pltpu.VMEM((9, c, pixels), f32),
            dma, dma((pieces,)), dma((pieces,)), dma((pieces,)), dma((pieces,)), dma((pieces,)), dma, dma,
            dma, dma, dma, dma, dma((n,)), dma((n,)), dma((n,)), dma((n,)),
            dma((sums,)), dma((sums,)), dma((sums,)), dma((sums,)), dma((sums,)), dma((sums,)),
        ],
        compiler_params=pltpu.CompilerParams(
            collective_id=0, has_side_effects=True, vmem_limit_bytes=limit
        ),
        name="video_conv",
    )(by_frame(features), pltpu.with_memory_space_constraint(jnp.transpose(kernel, (1, 0, 2)), pltpu.HBM), by_frame(cotangent))
    kernel_grad = pl.pallas_call(
        functools.partial(finish, scale),
        out_shape=jax.ShapeDtypeStruct((27, c, full), f32),
        in_specs=[vmem, vmem],
        out_specs=pl.BlockSpec(memory_space=pltpu.HBM),
        scratch_shapes=[pltpu.VMEM((27, c, full), f32), dma((9,))],
        compiler_params=pltpu.CompilerParams(vmem_limit_bytes=8 * 2**20 + kernel.size * 4),
        name="kernel_grad",
    )(mine, theirs)
    return back(conv_out), back(feature_grad), jnp.transpose(kernel_grad, (1, 0, 2))


def solution(mesh):
    def chosen(features, kernel, cotangent):
        if fits(mesh, features, kernel):
            return fused(mesh, features, kernel, cotangent)
        return local(features, kernel, cotangent)

    return jax.shard_map(
        chosen,
        mesh=mesh,
        in_specs=(
            P("chan", ("groups", "dp"), "tm", None),
            P("chan", None, None),
            P("chan", ("groups", "dp"), "tm", None),
        ),
        out_specs=(
            P("chan", ("groups", "dp"), "tm", None),
            P("chan", ("groups", "dp"), "tm", None),
            P(("groups", "chan"), None, None),
        ),
        check_vma=False,
    )
```

```python
import functools
import math

import jax
import jax.numpy as jnp
from jax import lax
from jax.experimental import pallas as pl
from jax.experimental.pallas import tpu as pltpu
from jax.sharding import PartitionSpec as P

WID = 64


def from_behind(x, axis, by):
    size = lax.axis_size(axis)
    pairs = [(i, i + by) for i in range(size) if 0 <= i + by < size]
    return lax.ppermute(x, axis, pairs)


def padded_copies(block):
    pixels = block.shape[-1]
    column = lax.broadcasted_iota(jnp.int32, (pixels,), 0) % WID
    nothing = jnp.zeros((), block.dtype)
    widths = [(0, 0), (0, 0), (0, 0), (WID + 1, WID + 1)]
    left_cut = jnp.pad(jnp.where(column == WID - 1, nothing, block), widths)
    untouched = jnp.pad(block, widths)
    right_cut = jnp.pad(jnp.where(column == 0, nothing, block), widths)
    return (left_cut, untouched, right_cut)


def tap_window(copies, first_frame, vertical, horizontal, frames, pixels):
    source = copies[horizontal]
    offset = vertical * WID + horizontal
    return source[:, :, first_frame : first_frame + frames, offset : offset + pixels]


def stacked_taps(copies, first_frame, flipped, frames, pixels):
    pieces = []
    for vertical in range(3):
        for horizontal in range(3):
            if flipped:
                pieces.append(
                    tap_window(copies, first_frame, 2 - vertical, 2 - horizontal, frames, pixels)
                )
            else:
                pieces.append(tap_window(copies, first_frame, vertical, horizontal, frames, pixels))
    concatenated = jnp.concatenate(pieces, axis=0)
    return concatenated.reshape(concatenated.shape[0], -1)


def local(features, kernel, cotangent):
    channels, clip_count, frames, pixels = features.shape
    flat_length = clip_count * frames * pixels
    widened = features.astype(jnp.float32)
    logistic = jax.nn.sigmoid(widened)
    activation = (widened * logistic).astype(jnp.bfloat16)
    slope_factor = logistic * (1.0 + widened * (1.0 - logistic))
    earlier = from_behind(activation[:, :, frames - 2 :, :], "tm", 1)
    extended = jnp.concatenate([earlier, activation], axis=2)
    upcoming = from_behind(cotangent[:, :, :2, :], "tm", -1)
    later_padded = jnp.concatenate([cotangent, upcoming], axis=2)
    cotangent_rows = cotangent.reshape(channels, -1)
    portion = lax.all_gather(extended, "chan", axis=0, tiled=True)
    out_sum = jnp.zeros((channels, flat_length), jnp.float32)
    amount = portion.shape[0]
    copies = padded_copies(portion)
    kernel_cols = kernel
    grad_parts = []
    for forward_temporal in range(3):
        stacked = stacked_taps(copies, forward_temporal, False, frames, pixels)
        weights = kernel_cols[:, 9 * forward_temporal : 9 * forward_temporal + 9, :].reshape(
            channels, 9 * amount
        )
        out_sum = out_sum + jnp.dot(weights, stacked, preferred_element_type=jnp.float32)
        grad_parts.append(
            lax.dot_general(
                cotangent_rows,
                stacked,
                (((1,), (1,)), ((), ())),
                preferred_element_type=jnp.float32,
            ).reshape(channels, 9, amount)
        )
    grad_sum = jnp.concatenate(grad_parts, axis=1)
    out_sum, grad_sum = (out_sum, grad_sum)
    conv_out = out_sum.reshape(features.shape).astype(jnp.bfloat16)
    position_count = lax.axis_size("dp") * lax.axis_size("tm") * flat_length
    kernel_grad = lax.psum(grad_sum, ("tm", "dp")) * (1.0 / math.sqrt(position_count))
    padded_later = padded_copies(later_padded)
    later_stacks = [
        stacked_taps(padded_later, 2 - temporal, True, frames, pixels) for temporal in range(3)
    ]
    amount = channels * lax.axis_size("chan")
    kernel_cols = kernel
    summed = jnp.zeros((amount, flat_length), jnp.float32)
    for temporal in range(3):
        weights = jnp.transpose(
            kernel_cols[:, 9 * temporal : 9 * temporal + 9, :], (2, 1, 0)
        ).reshape(amount, 9 * channels)
        summed = summed + jnp.dot(
            weights, later_stacks[temporal], preferred_element_type=jnp.float32
        )
    before_slope = lax.psum_scatter(
        summed.reshape(amount, clip_count, frames, pixels), "chan", scatter_dimension=0, tiled=True
    )
    feature_grad = (before_slope * slope_factor).astype(jnp.bfloat16)
    return (conv_out, feature_grad, kernel_grad)


def moved(x, rows, columns, pixels):
    step = rows * WID + columns
    place = lax.broadcasted_iota(jnp.int32, x.shape, len(x.shape) - 1)
    row, column = place // WID + rows, place % WID + columns
    out = x if step == 0 else pltpu.roll(x, (-step) % pixels, len(x.shape) - 1)
    inside = None
    if rows:
        inside = (row >= 0) & (row < pixels // WID)
    if columns:
        within = (column >= 0) & (column < WID)
        inside = within if inside is None else inside & within
    return out if inside is None else jnp.where(inside, out, 0.0)


def silu(x):
    wide = x.astype(jnp.float32)
    return wide * jax.nn.sigmoid(wide)


def body(
    sizes,
    f_hbm, w_hbm, g_hbm,
    out_ref, fg_ref, kg_ref,
    f_raw, g_raw, f_ref, g_ref, w_ref, stack, turned, act, cot_in, part, right_in, left_in, taps, frames_out, mine, theirs,
    f_sem, g_sem, w_sem, gather_right, gather_left, gather_recv, pair_send, pair_recv, own_send, own_recv,
    cot_send, cot_recv, halo_send, halo_recv, right_send, right_recv, left_send, left_recv,
    sum_send, sum_recv, keep_send, keep_recv, done_send, done_recv,
):
    n, lanes, rows, scale = sizes
    c, frames, pixels = f_raw.shape
    full = c * n
    half = c // 2
    long = frames * pixels
    every = 2 * frames
    per = c // rows
    total_pieces = per * n
    spare = lanes - c
    thirds = c // spare
    extra = 9 // (thirds + 1)
    kept = 9 - extra
    z, t, d = lax.axis_index("chan"), lax.axis_index("tm"), lax.axis_index("dp")

    def remote(src, dst, send, recv, **where):
        return pltpu.make_async_remote_copy(
            src_ref=src, dst_ref=dst, send_sem=send, recv_sem=recv,
            device_id=where, device_id_type=pl.DeviceIdType.MESH,
        )

    barrier = pltpu.get_barrier_semaphore()

    def greet(**where):
        pl.semaphore_signal(barrier, inc=1, device_id=where, device_id_type=pl.DeviceIdType.MESH)

    greet(dp=1 - d)

    @pl.when(z < n - 1)
    def _():
        greet(chan=z + 1)

    @pl.when(z > 0)
    def _():
        greet(chan=z - 1)

    greet(tm=1 - t)
    load_f = pltpu.make_async_copy(f_hbm, f_raw, f_sem)
    load_g = pltpu.make_async_copy(g_hbm, g_raw, g_sem)
    load_w = pltpu.make_async_copy(w_hbm, w_ref, w_sem)
    load_g.start()
    load_f.start()
    load_w.start()

    def half_rows(which):
        return pl.ds(pl.multiple_of(which * half, half), half)

    def frame_lanes(s):
        return pl.ds(pl.multiple_of(s * pixels, pixels), pixels)

    def own_lanes(which):
        return pl.ds(pl.multiple_of((which * frames + 2) * pixels, pixels), long)

    def shard_rows(q):
        return pl.ds(pl.multiple_of(q * c, c), c)

    def piece(p, which):
        return act.at[pl.ds(pl.multiple_of(p * rows, rows), rows), own_lanes(which)]

    def stack_frame(x, s, at):
        wide = x.astype(jnp.float32)
        for i in range(3):
            for j in range(3):
                stack[3 * i + j, at, frame_lanes(s)] = moved(wide, 1 - i, 1 - j, pixels).astype(jnp.bfloat16)

    everything = pl.ds(0, c)

    def own_frame(s, _):
        stack_frame(g_ref[s], t * frames + s, everything)
        return 0

    act[:, 0 : 2 * pixels] = jnp.zeros((full, 2 * pixels), jnp.bfloat16)
    stack[:, :, every * pixels : (every + 2) * pixels] = jnp.zeros((9, c, 2 * pixels), jnp.bfloat16)
    load_g.wait()
    g_ref[...] = jnp.transpose(g_raw[...], (1, 0, 2))
    load_f.wait()
    f_ref[...] = jnp.transpose(f_raw[...], (1, 0, 2))
    for s in range(frames):
        act[shard_rows(z), frame_lanes(t * frames + s + 2)] = silu(f_ref[s]).astype(jnp.bfloat16)
    lax.fori_loop(0, frames, own_frame, 0)

    @pl.when((z > 0) & (z < n - 1))
    def _():
        pl.semaphore_wait(barrier, 4)

    @pl.when((z == 0) | (z == n - 1))
    def _():
        pl.semaphore_wait(barrier, 3)

    def pass_right(p):
        return remote(piece(p, t), piece(p, t), gather_right.at[p], gather_recv.at[p], chan=z + 1)

    def pass_left(p):
        return remote(piece(p, t), piece(p, t), gather_left.at[p], gather_recv.at[p], chan=z - 1)

    def pair_copy(p, which):
        return remote(piece(p, which), piece(p, which), pair_send.at[p], pair_recv.at[p], tm=1 - t)

    def own_copy(which):
        place = act.at[shard_rows(z), own_lanes(which)]
        return remote(place, place, own_send, own_recv, tm=1 - t)

    def cot_copy():
        return remote(
            g_ref.at[:, half_rows(1 - t)], cot_in.at[:, half_rows(1 - t)], cot_send, cot_recv, tm=1 - t
        )

    def halo_copy():
        return remote(
            g_ref.at[pl.ds(0, 2), half_rows(1)], cot_in.at[pl.ds(0, 2), half_rows(1)], halo_send, halo_recv, tm=1 - t
        )

    cot_copy().start()
    own_copy(t).start()

    @pl.when(t == 1)
    def _():
        halo_copy().start()

    for k in range(per):
        @pl.when(z < n - 1)
        def _():
            pass_right(z * per + per - 1 - k).start()

        @pl.when(z > 0)
        def _():
            pass_left(z * per + k).start()

    def other_frame(s, _):
        stack_frame(cot_in[s, half_rows(t), :], (1 - t) * frames + s, half_rows(t))
        return 0

    def tick(k):
        @pl.when((z + 1) * per + k < total_pieces)
        def _():
            p = (z + 1) * per + k
            pass_left(p).wait_recv()

            @pl.when(z > 0)
            def _():
                pass_left(p).start()

            pair_copy(p, t).start()

        @pl.when(z * per - 1 - k >= 0)
        def _():
            p = z * per - 1 - k
            pass_right(p).wait_recv()

            @pl.when(z < n - 1)
            def _():
                pass_right(p).start()

            pair_copy(p, t).start()

    def pair_tick(k):
        @pl.when((z + 1) * per + k < total_pieces)
        def _():
            pair_copy((z + 1) * per + k, 1 - t).wait_recv()

        @pl.when(z * per - 1 - k >= 0)
        def _():
            pair_copy(z * per - 1 - k, 1 - t).wait_recv()

    def shard_of(i):
        near, far = z + 1 - 2 * (z // 2), (n - 1) - (n - 1) * (z // 2)
        return (z, near, 2 * (n - 1) - z - near - far, far)[i]

    def cell(ref, i, a, which):
        return ref.at[i, which, pl.ds(kept * a, kept)]

    def sum_copy(i, a):
        return remote(
            cell(mine, i, a, t), cell(theirs, i, a, t), sum_send.at[3 * i + a], sum_recv.at[3 * i + a], dp=1 - d
        )

    def keep_copy(i, a, which):
        place = cell(mine, i, a, which)
        return remote(place, place, keep_send.at[3 * i + a], keep_recv.at[3 * i + a], tm=1 - t)

    def done_copy(i, a, which):
        place = cell(theirs, i, a, which)
        return remote(place, place, done_send.at[3 * i + a], done_recv.at[3 * i + a], tm=1 - t)

    def lane_of(shape):
        return lax.broadcasted_iota(jnp.int32, shape, len(shape) - 1)

    def matched(held, channels):
        cut = held.shape[0] // 32 * 16
        return jnp.concatenate(
            [
                lax.dot_general(x, channels, (((1,), (1,)), ((), ())), preferred_element_type=jnp.float32)
                for x in (held[:cut], held[cut:])
            ],
            axis=0,
        )

    def send_terms(i, a, terms):
        last = terms[kept * half :]
        for h in range(thirds):
            block = terms[h * extra * half : (h + 1) * extra * half]
            block = jnp.where(lane_of(block.shape) < c, block, pltpu.roll(last, c - spare * h, 1))
            mine[i, t, kept * a + h * extra : kept * a + (h + 1) * extra] = block.reshape(
                extra, half, lanes
            ).astype(jnp.bfloat16)
        mine[i, t, kept * a + thirds * extra : kept * (a + 1)] = terms[thirds * extra * half : kept * half].reshape(
            kept - thirds * extra, half, lanes
        ).astype(jnp.bfloat16)
        sum_copy(i, a).start()

    def kernel_terms(i):
        at = shard_rows(shard_of(i))

        def channels(first, count):
            return [
                act[at, first * pixels : (first + count) * pixels],
                jnp.zeros((spare, count * pixels), jnp.bfloat16),
            ]

        def held(first):
            return stack[:, half_rows(t), first * pixels : every * pixels].reshape(9 * half, (every - first) * pixels)

        pair = matched(held(0), jnp.concatenate(channels(1, every) + channels(2, every), axis=0))
        send_terms(i, 1, pair[:, :lanes])
        send_terms(i, 2, pair[:, lanes:])
        send_terms(i, 0, matched(held(2), jnp.concatenate(channels(2, every - 2), axis=0)))
        for a in range(3):
            keep_copy(i, a, t).start()

    def assemble(i, a, which):
        at = shard_of(i) * c
        both = (
            mine[i, which, kept * a : kept * (a + 1)].astype(jnp.float32)
            + theirs[i, which, kept * a : kept * (a + 1)].astype(jnp.float32)
        ) * scale
        last = None
        for h in reversed(range(thirds)):
            block = pltpu.roll(both[h * extra : (h + 1) * extra].reshape(extra * half, lanes), spare * (h + 1), 1)
            last = block if last is None else jnp.where(lane_of(block.shape) < spare * (h + 1), block, last)
        whole = jnp.concatenate([both.reshape(kept * half, lanes), last], axis=0)
        start = at % lanes
        turned_lanes = pltpu.roll(whole, start, 1).reshape(9, half, lanes)
        lane = lane_of(turned_lanes.shape)
        tile = at // lanes

        def put(tile, inside):
            place = (pl.ds(9 * a, 9), half_rows(which), pl.ds(pl.multiple_of(tile * lanes, lanes), lanes))
            kg_ref[place] = jnp.where(inside, turned_lanes, kg_ref[place])

        put(tile, (lane >= start) & (lane < start + c))

        @pl.when(start + c > lanes)
        def _():
            put(tile + 1, lane < start + c - lanes)

    def before(s):
        rhs = jnp.concatenate(
            [stack[:, :, frame_lanes(t * frames + s + 2 - a)].reshape(9 * c, pixels) for a in range(3)], axis=0
        )
        total = jnp.dot(turned[...], rhs, preferred_element_type=jnp.float32)
        for q in range(n):
            part[q, s] = total[q * c : (q + 1) * c].astype(jnp.bfloat16)

    few = frames // 2

    def share_right(q, h, src):
        at = pl.ds(h * few, few)
        return remote(src.at[q, at], right_in.at[q, at], right_send.at[2 * q + h], right_recv.at[2 * q + h], chan=z + 1)

    def share_left(q, h, src):
        at = pl.ds(h * few, few)
        return remote(src.at[q, at], left_in.at[q, at], left_send.at[2 * q + h], left_recv.at[2 * q + h], chan=z - 1)

    def first_share(j, h):
        @pl.when(z == 0)
        def _():
            share_right(n - 1 - j, h, part).start()

        @pl.when(z == n - 1)
        def _():
            share_left(j, h, part).start()

    def add_part(held, q, h):
        for s in range(h * few, (h + 1) * few):
            held[q, s] = (held[q, s].astype(jnp.float32) + part[q, s].astype(jnp.float32)).astype(jnp.bfloat16)

    def relay_right(q, h):
        share_right(q, h, right_in).wait_recv()
        add_part(right_in, q, h)
        share_right(q, h, right_in).start()

    def relay_left(q, h):
        share_left(q, h, left_in).wait_recv()
        add_part(left_in, q, h)
        share_left(q, h, left_in).start()

    def relay(k):
        kind, h = ((0, 0), (0, 1), (2, 0), (1, 0), (2, 1), (1, 1))[k]

        @pl.when(z == 1)
        def _():
            if kind == 2:
                relay_left(0, h)
            else:
                relay_right(n - 1 - kind, h)

        @pl.when(z == 2)
        def _():
            if kind == 2:
                relay_right(n - 1, h)
            else:
                relay_left(kind, h)

    def convolve(u):
        rhs = jnp.concatenate([act[:, frame_lanes(t * frames + u + a)] for a in range(3)], axis=0)
        lhs = jnp.concatenate([w_ref[9 * a : 9 * a + 9].reshape(9 * c, full) for a in range(3)], axis=1)
        taps[...] = jnp.dot(lhs, rhs, preferred_element_type=jnp.float32).reshape(9, c, pixels)
        result = jnp.zeros((c, pixels), jnp.float32)
        for i in range(3):
            for j in range(3):
                result = result + moved(taps[3 * i + j], i - 1, j - 1, pixels)
        frames_out[u] = result.astype(jnp.bfloat16)

    def forward(i):
        for a in (1, 2, 0):
            sum_copy(i, a).wait_recv()
            done_copy(i, a, t).start()
            assemble(i, a, t)

    def complete(i):
        for a in (1, 2, 0):
            keep_copy(i, a, 1 - t).wait_recv()
            done_copy(i, a, 1 - t).wait_recv()
            assemble(i, a, 1 - t)

    cot_copy().wait_recv()
    lax.fori_loop(0, frames, other_frame, 0)
    own_copy(1 - t).wait_recv()
    kernel_terms(0)

    @pl.when(t == 0)
    def _():
        halo_copy().wait_recv()

        def next_frame(s, _):
            stack_frame(cot_in[s, half_rows(1), :], frames + s, half_rows(1))
            return 0

        lax.fori_loop(0, 2, next_frame, 0)

    load_w.wait()
    turned[...] = jnp.transpose(w_ref[...].reshape(27 * c, full))
    before(0)
    before(1)
    first_share(0, 0)
    tick(0)
    before(2)
    before(3)
    first_share(0, 1)
    for j in range(1, n - 1):
        for h in range(2):
            first_share(j, h)
    tick(1)
    tick(2)
    for k in (0, 1, 2):
        pair_tick(k)
    kernel_terms(1)
    tick(3)
    tick(4)
    relay(0)
    tick(5)
    for k in (3, 4, 5):
        pair_tick(k)
    kernel_terms(2)
    relay(1)
    tick(6)
    forward(0)
    tick(7)
    relay(2)
    tick(8)
    for k in (6, 7, 8):
        pair_tick(k)
    kernel_terms(3)
    relay(3)
    relay(4)
    relay(5)
    complete(0)
    for u in range(frames):
        convolve(u)
    out_ref[...] = jnp.transpose(frames_out[...], (1, 0, 2))
    forward(1)
    complete(1)

    for h in range(2):
        @pl.when(z > 0)
        def _():
            share_right(z, h, right_in).wait_recv()

        @pl.when(z < n - 1)
        def _():
            share_left(z, h, left_in).wait_recv()

    def slope_frame(s, _):
        wide = f_ref[s].astype(jnp.float32)
        logistic = jax.nn.sigmoid(wide)
        slope = logistic * (1.0 + wide * (1.0 - logistic))

        def keep(total):
            frames_out[s] = (total * slope).astype(jnp.bfloat16)

        own = part[z, s].astype(jnp.float32)

        @pl.when(z == 0)
        def _():
            keep(own + left_in[z, s].astype(jnp.float32))

        @pl.when(z == n - 1)
        def _():
            keep(own + right_in[z, s].astype(jnp.float32))

        @pl.when((z > 0) & (z < n - 1))
        def _():
            keep(own + (left_in[z, s].astype(jnp.float32) + right_in[z, s].astype(jnp.float32)))

        return 0

    lax.fori_loop(0, frames, slope_frame, 0)
    fg_ref[...] = jnp.transpose(frames_out[...], (1, 0, 2))
    forward(2)
    complete(2)

    for p in range(total_pieces):
        @pl.when((z < n - 1) & (p < (z + 1) * per))
        def _():
            pass_right(p).wait_send()

        @pl.when((z > 0) & (p >= z * per))
        def _():
            pass_left(p).wait_send()

        @pl.when((p < z * per) | (p >= (z + 1) * per))
        def _():
            pair_copy(p, t).wait_send()

    for h in range(2):
        for j in range(n - 1):
            @pl.when(z < n - 1 - j)
            def _():
                share_right(n - 1 - j, h, right_in).wait_send()

            @pl.when(z > j)
            def _():
                share_left(j, h, left_in).wait_send()

    own_copy(t).wait_send()
    cot_copy().wait_send()

    @pl.when(t == 1)
    def _():
        halo_copy().wait_send()

    for i in range(n - 1):
        for a in range(3):
            sum_copy(i, a).wait_send()
            keep_copy(i, a, t).wait_send()
            done_copy(i, a, t).wait_send()

    forward(n - 1)
    complete(n - 1)
    for a in range(3):
        sum_copy(n - 1, a).wait_send()
        keep_copy(n - 1, a, t).wait_send()
        done_copy(n - 1, a, t).wait_send()


def write(out_ref, fg_ref, kg_ref, out_hbm, fg_hbm, kg_hbm, sems):
    copies = [
        pltpu.make_async_copy(kg_ref, kg_hbm, sems.at[0]),
        pltpu.make_async_copy(out_ref, out_hbm, sems.at[1]),
        pltpu.make_async_copy(fg_ref, fg_hbm, sems.at[2]),
    ]
    for copy in copies:
        copy.start()
    for copy in copies:
        copy.wait()


LANES = 128


def fits(mesh, features, kernel):
    c, clips, frames, pixels = features.shape
    return (
        mesh.shape["tm"] == 2
        and mesh.shape["chan"] == 4
        and mesh.shape["dp"] == 2
        and clips == 1
        and frames == 4
        and c * mesh.shape["chan"] == kernel.shape[2]
        and kernel.shape[2] == 3 * LANES
        and pixels % 128 == 0
        and pixels % WID == 0
        and kernel.size * 24 + features.size * 96 < 56 * 2**20
    )


def fused(mesh, features, kernel, cotangent):
    c, clips, frames, pixels = features.shape
    n = mesh.shape["chan"]
    full = c * n
    scale = 1.0 / math.sqrt(mesh.shape["dp"] * mesh.shape["tm"] * clips * frames * pixels)
    vmem = pl.BlockSpec(memory_space=pltpu.VMEM)
    hbm = pl.BlockSpec(memory_space=pltpu.HBM)
    b16, f32 = jnp.bfloat16, jnp.float32
    dma = pltpu.SemaphoreType.DMA
    half = c // 2
    rows = math.gcd(c, LANES)
    pieces = full // rows
    sums = 3 * n
    spare = LANES - c
    kept = 9 - 9 // (c // spare + 1)
    limit = 8 * 2**20 + kernel.size * 22 + features.size * 64
    in_hbm = lambda x: pltpu.with_memory_space_constraint(x, pltpu.HBM)
    shards = pltpu.VMEM((n, frames, c, pixels), b16)
    by_frame = pltpu.VMEM((frames, c, pixels), b16)
    by_channel = pltpu.VMEM((c, frames, pixels), b16)
    halves = pltpu.VMEM((n, 2, 3 * kept, half, LANES), b16)
    shapes = (
        jax.ShapeDtypeStruct((c, frames, pixels), b16),
        jax.ShapeDtypeStruct((c, frames, pixels), b16),
        jax.ShapeDtypeStruct((27, c, full), f32),
    )
    held = pl.pallas_call(
        functools.partial(body, (n, LANES, rows, scale)),
        out_shape=shapes,
        in_specs=[hbm, hbm, hbm],
        out_specs=(vmem,) * 3,
        scratch_shapes=[
            by_channel, by_channel, by_frame, by_frame,
            pltpu.VMEM((27, c, full), b16),
            pltpu.VMEM((9, c, (2 * frames + 2) * pixels), b16),
            pltpu.VMEM((full, 27 * c), b16),
            pltpu.VMEM((full, (2 * frames + 2) * pixels), b16),
            by_frame,
            shards, shards, shards,
            pltpu.VMEM((9, c, pixels), f32),
            by_frame,
            halves, halves,
            dma, dma, dma, dma((pieces,)), dma((pieces,)), dma((pieces,)), dma((pieces,)), dma((pieces,)), dma, dma,
            dma, dma, dma, dma, dma((2 * n,)), dma((2 * n,)), dma((2 * n,)), dma((2 * n,)),
            dma((sums,)), dma((sums,)), dma((sums,)), dma((sums,)), dma((sums,)), dma((sums,)),
        ],
        compiler_params=pltpu.CompilerParams(
            collective_id=0, has_side_effects=True, vmem_limit_bytes=limit
        ),
        name="video_conv",
    )(
        in_hbm(features.reshape(c, frames, pixels)),
        in_hbm(jnp.transpose(kernel, (1, 0, 2))),
        in_hbm(cotangent.reshape(c, frames, pixels)),
    )
    conv_out, feature_grad, kernel_grad = pl.pallas_call(
        write,
        out_shape=shapes,
        in_specs=[vmem] * 3,
        out_specs=(hbm,) * 3,
        scratch_shapes=[dma((3,))],
        compiler_params=pltpu.CompilerParams(vmem_limit_bytes=12 * 2**20),
        name="write",
    )(*held)
    return conv_out.reshape(features.shape), feature_grad.reshape(features.shape), jnp.transpose(kernel_grad, (1, 0, 2))


def solution(mesh):
    def chosen(features, kernel, cotangent):
        if fits(mesh, features, kernel):
            return fused(mesh, features, kernel, cotangent)
        return local(features, kernel, cotangent)

    return jax.shard_map(
        chosen,
        mesh=mesh,
        in_specs=(
            P("chan", ("groups", "dp"), "tm", None),
            P("chan", None, None),
            P("chan", ("groups", "dp"), "tm", None),
        ),
        out_specs=(
            P("chan", ("groups", "dp"), "tm", None),
            P("chan", ("groups", "dp"), "tm", None),
            P(("groups", "chan"), None, None),
        ),
        check_vma=False,
    )
```

```python
import functools
import math

import jax
import jax.numpy as jnp
from jax import lax
from jax.experimental import pallas as pl
from jax.experimental.pallas import tpu as pltpu
from jax.sharding import PartitionSpec as P

WID = 64


def from_behind(x, axis, by):
    size = lax.axis_size(axis)
    pairs = [(i, i + by) for i in range(size) if 0 <= i + by < size]
    return lax.ppermute(x, axis, pairs)


def padded_copies(block):
    pixels = block.shape[-1]
    column = lax.broadcasted_iota(jnp.int32, (pixels,), 0) % WID
    nothing = jnp.zeros((), block.dtype)
    widths = [(0, 0), (0, 0), (0, 0), (WID + 1, WID + 1)]
    left_cut = jnp.pad(jnp.where(column == WID - 1, nothing, block), widths)
    untouched = jnp.pad(block, widths)
    right_cut = jnp.pad(jnp.where(column == 0, nothing, block), widths)
    return (left_cut, untouched, right_cut)


def tap_window(copies, first_frame, vertical, horizontal, frames, pixels):
    source = copies[horizontal]
    offset = vertical * WID + horizontal
    return source[:, :, first_frame : first_frame + frames, offset : offset + pixels]


def stacked_taps(copies, first_frame, flipped, frames, pixels):
    pieces = []
    for vertical in range(3):
        for horizontal in range(3):
            if flipped:
                pieces.append(
                    tap_window(copies, first_frame, 2 - vertical, 2 - horizontal, frames, pixels)
                )
            else:
                pieces.append(tap_window(copies, first_frame, vertical, horizontal, frames, pixels))
    concatenated = jnp.concatenate(pieces, axis=0)
    return concatenated.reshape(concatenated.shape[0], -1)


def local(features, kernel, cotangent):
    channels, clip_count, frames, pixels = features.shape
    flat_length = clip_count * frames * pixels
    widened = features.astype(jnp.float32)
    logistic = jax.nn.sigmoid(widened)
    activation = (widened * logistic).astype(jnp.bfloat16)
    slope_factor = logistic * (1.0 + widened * (1.0 - logistic))
    earlier = from_behind(activation[:, :, frames - 2 :, :], "tm", 1)
    extended = jnp.concatenate([earlier, activation], axis=2)
    upcoming = from_behind(cotangent[:, :, :2, :], "tm", -1)
    later_padded = jnp.concatenate([cotangent, upcoming], axis=2)
    cotangent_rows = cotangent.reshape(channels, -1)
    portion = lax.all_gather(extended, "chan", axis=0, tiled=True)
    out_sum = jnp.zeros((channels, flat_length), jnp.float32)
    amount = portion.shape[0]
    copies = padded_copies(portion)
    kernel_cols = kernel
    grad_parts = []
    for forward_temporal in range(3):
        stacked = stacked_taps(copies, forward_temporal, False, frames, pixels)
        weights = kernel_cols[:, 9 * forward_temporal : 9 * forward_temporal + 9, :].reshape(
            channels, 9 * amount
        )
        out_sum = out_sum + jnp.dot(weights, stacked, preferred_element_type=jnp.float32)
        grad_parts.append(
            lax.dot_general(
                cotangent_rows,
                stacked,
                (((1,), (1,)), ((), ())),
                preferred_element_type=jnp.float32,
            ).reshape(channels, 9, amount)
        )
    grad_sum = jnp.concatenate(grad_parts, axis=1)
    out_sum, grad_sum = (out_sum, grad_sum)
    conv_out = out_sum.reshape(features.shape).astype(jnp.bfloat16)
    position_count = lax.axis_size("dp") * lax.axis_size("tm") * flat_length
    kernel_grad = lax.psum(grad_sum, ("tm", "dp")) * (1.0 / math.sqrt(position_count))
    padded_later = padded_copies(later_padded)
    later_stacks = [
        stacked_taps(padded_later, 2 - temporal, True, frames, pixels) for temporal in range(3)
    ]
    amount = channels * lax.axis_size("chan")
    kernel_cols = kernel
    summed = jnp.zeros((amount, flat_length), jnp.float32)
    for temporal in range(3):
        weights = jnp.transpose(
            kernel_cols[:, 9 * temporal : 9 * temporal + 9, :], (2, 1, 0)
        ).reshape(amount, 9 * channels)
        summed = summed + jnp.dot(
            weights, later_stacks[temporal], preferred_element_type=jnp.float32
        )
    before_slope = lax.psum_scatter(
        summed.reshape(amount, clip_count, frames, pixels), "chan", scatter_dimension=0, tiled=True
    )
    feature_grad = (before_slope * slope_factor).astype(jnp.bfloat16)
    return (conv_out, feature_grad, kernel_grad)


def moved(x, rows, columns, pixels):
    step = rows * WID + columns
    place = lax.broadcasted_iota(jnp.int32, (1, pixels), 1)
    row, column = place // WID + rows, place % WID + columns
    out = x if step == 0 else pltpu.roll(x, (-step) % pixels, len(x.shape) - 1)
    inside = None
    if rows:
        inside = (row >= 0) & (row < pixels // WID)
    if columns:
        within = (column >= 0) & (column < WID)
        inside = within if inside is None else inside & within
    return out if inside is None else out * jnp.where(inside, 1.0, 0.0)


def silu(x):
    wide = x.astype(jnp.float32)
    return wide * jax.nn.sigmoid(wide)


def body(
    sizes,
    f_hbm, w_hbm, g_hbm,
    out_ref, fg_ref, kg_ref,
    f_raw, g_raw, f_ref, g_ref, w_ref, stack, turned, act, cot_in, part, right_in, left_in, taps, frames_out, mine, theirs,
    f_sem, g_sem, w_sem, gather_right, gather_left, gather_recv, pair_send, pair_recv, own_send, own_recv,
    cot_send, cot_recv, halo_send, halo_recv, right_send, right_recv, left_send, left_recv,
    sum_send, sum_recv, keep_send, keep_recv, done_send, done_recv,
):
    n, lanes, rows, scale = sizes
    c, frames, pixels = f_raw.shape
    full = c * n
    half = c // 2
    long = frames * pixels
    every = 2 * frames
    per = c // rows
    total_pieces = per * n
    spare = lanes - c
    thirds = c // spare
    extra = 9 // (thirds + 1)
    kept = 9 - extra
    z, t, d = lax.axis_index("chan"), lax.axis_index("tm"), lax.axis_index("dp")

    def remote(src, dst, send, recv, **where):
        return pltpu.make_async_remote_copy(
            src_ref=src, dst_ref=dst, send_sem=send, recv_sem=recv,
            device_id=where, device_id_type=pl.DeviceIdType.MESH,
        )

    barrier = pltpu.get_barrier_semaphore()

    def greet(**where):
        pl.semaphore_signal(barrier, inc=1, device_id=where, device_id_type=pl.DeviceIdType.MESH)

    greet(dp=1 - d)

    @pl.when(z < n - 1)
    def _():
        greet(chan=z + 1)

    @pl.when(z > 0)
    def _():
        greet(chan=z - 1)

    greet(tm=1 - t)
    load_f = pltpu.make_async_copy(f_hbm, f_raw, f_sem)
    load_g = pltpu.make_async_copy(g_hbm, g_raw, g_sem)
    load_w = pltpu.make_async_copy(w_hbm, w_ref, w_sem)
    load_g.start()
    load_f.start()
    load_w.start()

    def half_rows(which):
        return pl.ds(pl.multiple_of(which * half, half), half)

    def frame_lanes(s):
        return pl.ds(pl.multiple_of(s * pixels, pixels), pixels)

    def own_lanes(which):
        return pl.ds(pl.multiple_of((which * frames + 2) * pixels, pixels), long)

    def shard_rows(q):
        return pl.ds(pl.multiple_of(q * c, c), c)

    def piece(p, which):
        return act.at[pl.ds(pl.multiple_of(p * rows, rows), rows), own_lanes(which)]

    def stack_frame(x, s, at):
        wide = x.astype(jnp.float32)
        for i in range(3):
            for j in range(3):
                stack[3 * i + j, at, frame_lanes(s)] = moved(wide, 1 - i, 1 - j, pixels).astype(jnp.bfloat16)

    everything = pl.ds(0, c)

    def own_frame(s, _):
        stack_frame(g_ref[s], t * frames + s, everything)
        return 0

    act[:, 0 : 2 * pixels] = jnp.zeros((full, 2 * pixels), jnp.bfloat16)
    stack[:, :, every * pixels : (every + 2) * pixels] = jnp.zeros((9, c, 2 * pixels), jnp.bfloat16)
    load_g.wait()
    g_ref[...] = jnp.transpose(g_raw[...], (1, 0, 2))
    load_f.wait()
    f_ref[...] = jnp.transpose(f_raw[...], (1, 0, 2))
    for s in range(frames):
        act[shard_rows(z), frame_lanes(t * frames + s + 2)] = silu(f_ref[s]).astype(jnp.bfloat16)
    lax.fori_loop(0, frames, own_frame, 0)

    @pl.when((z > 0) & (z < n - 1))
    def _():
        pl.semaphore_wait(barrier, 4)

    @pl.when((z == 0) | (z == n - 1))
    def _():
        pl.semaphore_wait(barrier, 3)

    def pass_right(p):
        return remote(piece(p, t), piece(p, t), gather_right.at[p], gather_recv.at[p], chan=z + 1)

    def pass_left(p):
        return remote(piece(p, t), piece(p, t), gather_left.at[p], gather_recv.at[p], chan=z - 1)

    def pair_copy(p, which):
        return remote(piece(p, which), piece(p, which), pair_send.at[p], pair_recv.at[p], tm=1 - t)

    def own_copy(which):
        place = act.at[shard_rows(z), own_lanes(which)]
        return remote(place, place, own_send, own_recv, tm=1 - t)

    def cot_copy():
        return remote(
            g_ref.at[:, half_rows(1 - t)], cot_in.at[:, half_rows(1 - t)], cot_send, cot_recv, tm=1 - t
        )

    def halo_copy():
        return remote(
            g_ref.at[pl.ds(0, 2), half_rows(1)], cot_in.at[pl.ds(0, 2), half_rows(1)], halo_send, halo_recv, tm=1 - t
        )

    cot_copy().start()
    own_copy(t).start()

    @pl.when(t == 1)
    def _():
        halo_copy().start()

    for k in range(per):
        @pl.when(z < n - 1)
        def _():
            pass_right(z * per + per - 1 - k).start()

        @pl.when(z > 0)
        def _():
            pass_left(z * per + k).start()

    def other_frame(s, _):
        stack_frame(cot_in[s, half_rows(t), :], (1 - t) * frames + s, half_rows(t))
        return 0

    def tick(k):
        @pl.when((z + 1) * per + k < total_pieces)
        def _():
            p = (z + 1) * per + k
            pass_left(p).wait_recv()

            @pl.when(z > 0)
            def _():
                pass_left(p).start()

            pair_copy(p, t).start()

        @pl.when(z * per - 1 - k >= 0)
        def _():
            p = z * per - 1 - k
            pass_right(p).wait_recv()

            @pl.when(z < n - 1)
            def _():
                pass_right(p).start()

            pair_copy(p, t).start()

    def pair_tick(k):
        @pl.when((z + 1) * per + k < total_pieces)
        def _():
            pair_copy((z + 1) * per + k, 1 - t).wait_recv()

        @pl.when(z * per - 1 - k >= 0)
        def _():
            pair_copy(z * per - 1 - k, 1 - t).wait_recv()

    def shard_of(i):
        near, far = z + 1 - 2 * (z // 2), (n - 1) - (n - 1) * (z // 2)
        return (z, near, 2 * (n - 1) - z - near - far, far)[i]

    def cell(ref, i, a, which):
        return ref.at[i, which, pl.ds(kept * a, kept)]

    def sum_copy(i, a):
        return remote(
            cell(mine, i, a, t), cell(theirs, i, a, t), sum_send.at[3 * i + a], sum_recv.at[3 * i + a], dp=1 - d
        )

    def keep_copy(i, a, which):
        place = cell(mine, i, a, which)
        return remote(place, place, keep_send.at[3 * i + a], keep_recv.at[3 * i + a], tm=1 - t)

    def done_copy(i, a, which):
        place = cell(theirs, i, a, which)
        return remote(place, place, done_send.at[3 * i + a], done_recv.at[3 * i + a], tm=1 - t)

    def lane_of(shape):
        return lax.broadcasted_iota(jnp.int32, shape, len(shape) - 1)

    def matched(held, channels):
        cut = held.shape[0] // 32 * 16
        return jnp.concatenate(
            [
                lax.dot_general(x, channels, (((1,), (1,)), ((), ())), preferred_element_type=jnp.float32)
                for x in (held[:cut], held[cut:])
            ],
            axis=0,
        )

    def send_terms(i, a, terms):
        last = terms[kept * half :]
        for h in range(thirds):
            block = terms[h * extra * half : (h + 1) * extra * half]
            block = jnp.where(lane_of(block.shape) < c, block, pltpu.roll(last, c - spare * h, 1))
            mine[i, t, kept * a + h * extra : kept * a + (h + 1) * extra] = block.reshape(
                extra, half, lanes
            ).astype(jnp.bfloat16)
        mine[i, t, kept * a + thirds * extra : kept * (a + 1)] = terms[thirds * extra * half : kept * half].reshape(
            kept - thirds * extra, half, lanes
        ).astype(jnp.bfloat16)
        sum_copy(i, a).start()

    def kernel_terms(i):
        at = shard_rows(shard_of(i))

        def channels(first, count):
            return [
                act[at, first * pixels : (first + count) * pixels],
                jnp.zeros((spare, count * pixels), jnp.bfloat16),
            ]

        def held(first):
            return stack[:, half_rows(t), first * pixels : every * pixels].reshape(9 * half, (every - first) * pixels)

        pair = matched(held(0), jnp.concatenate(channels(1, every) + channels(2, every), axis=0))
        send_terms(i, 1, pair[:, :lanes])
        send_terms(i, 2, pair[:, lanes:])
        send_terms(i, 0, matched(held(2), jnp.concatenate(channels(2, every - 2), axis=0)))
        for a in range(3):
            keep_copy(i, a, t).start()

    def assemble(i, a, which):
        at = shard_of(i) * c
        both = (
            mine[i, which, kept * a : kept * (a + 1)].astype(jnp.float32)
            + theirs[i, which, kept * a : kept * (a + 1)].astype(jnp.float32)
        ) * scale
        last = None
        for h in reversed(range(thirds)):
            block = pltpu.roll(both[h * extra : (h + 1) * extra].reshape(extra * half, lanes), spare * (h + 1), 1)
            last = block if last is None else jnp.where(lane_of(block.shape) < spare * (h + 1), block, last)
        whole = jnp.concatenate([both.reshape(kept * half, lanes), last], axis=0)
        start = at % lanes
        turned_lanes = pltpu.roll(whole, start, 1).reshape(9, half, lanes)
        lane = lane_of(turned_lanes.shape)
        tile = at // lanes

        def put(tile, inside):
            place = (pl.ds(9 * a, 9), half_rows(which), pl.ds(pl.multiple_of(tile * lanes, lanes), lanes))
            kg_ref[place] = jnp.where(inside, turned_lanes, kg_ref[place])

        put(tile, (lane >= start) & (lane < start + c))

        @pl.when(start + c > lanes)
        def _():
            put(tile + 1, lane < start + c - lanes)

    def before(s):
        rhs = jnp.concatenate(
            [stack[:, :, frame_lanes(t * frames + s + 2 - a)].reshape(9 * c, pixels) for a in range(3)], axis=0
        )
        total = jnp.dot(turned[...], rhs, preferred_element_type=jnp.float32)
        for q in range(n):
            part[q, s] = total[q * c : (q + 1) * c].astype(jnp.bfloat16)

    few = frames // 2

    def share_right(q, h, src):
        at = pl.ds(h * few, few)
        return remote(src.at[q, at], right_in.at[q, at], right_send.at[2 * q + h], right_recv.at[2 * q + h], chan=z + 1)

    def share_left(q, h, src):
        at = pl.ds(h * few, few)
        return remote(src.at[q, at], left_in.at[q, at], left_send.at[2 * q + h], left_recv.at[2 * q + h], chan=z - 1)

    def first_share(j, h):
        @pl.when(z == 0)
        def _():
            share_right(n - 1 - j, h, part).start()

        @pl.when(z == n - 1)
        def _():
            share_left(j, h, part).start()

    def add_part(held, q, h):
        for s in range(h * few, (h + 1) * few):
            held[q, s] = (held[q, s].astype(jnp.float32) + part[q, s].astype(jnp.float32)).astype(jnp.bfloat16)

    def relay_right(q, h):
        share_right(q, h, right_in).wait_recv()
        add_part(right_in, q, h)
        share_right(q, h, right_in).start()

    def relay_left(q, h):
        share_left(q, h, left_in).wait_recv()
        add_part(left_in, q, h)
        share_left(q, h, left_in).start()

    def relay(k):
        kind, h = ((0, 0), (0, 1), (2, 0), (1, 0), (2, 1), (1, 1))[k]

        @pl.when(z == 1)
        def _():
            if kind == 2:
                relay_left(0, h)
            else:
                relay_right(n - 1 - kind, h)

        @pl.when(z == 2)
        def _():
            if kind == 2:
                relay_right(n - 1, h)
            else:
                relay_left(kind, h)

    def convolve(u):
        rhs = jnp.concatenate([act[:, frame_lanes(t * frames + u + a)] for a in range(3)], axis=0)
        lhs = jnp.concatenate([w_ref[9 * a : 9 * a + 9].reshape(9 * c, full) for a in range(3)], axis=1)
        taps[...] = jnp.dot(lhs, rhs, preferred_element_type=jnp.float32).reshape(9, c, pixels)
        result = jnp.zeros((c, pixels), jnp.float32)
        for i in range(3):
            for j in range(3):
                result = result + moved(taps[3 * i + j], i - 1, j - 1, pixels)
        frames_out[u] = result.astype(jnp.bfloat16)

    def forward(i):
        for a in (1, 2, 0):
            sum_copy(i, a).wait_recv()
            done_copy(i, a, t).start()
            assemble(i, a, t)

    def complete(i):
        for a in (1, 2, 0):
            keep_copy(i, a, 1 - t).wait_recv()
            done_copy(i, a, 1 - t).wait_recv()
            assemble(i, a, 1 - t)

    cot_copy().wait_recv()
    lax.fori_loop(0, frames, other_frame, 0)
    own_copy(1 - t).wait_recv()
    kernel_terms(0)

    @pl.when(t == 0)
    def _():
        halo_copy().wait_recv()

        def next_frame(s, _):
            stack_frame(cot_in[s, half_rows(1), :], frames + s, half_rows(1))
            return 0

        lax.fori_loop(0, 2, next_frame, 0)

    load_w.wait()
    turned[...] = jnp.transpose(w_ref[...].reshape(27 * c, full))
    before(0)
    before(1)
    first_share(0, 0)
    tick(0)
    before(2)
    before(3)
    first_share(0, 1)
    for j in range(1, n - 1):
        for h in range(2):
            first_share(j, h)
    tick(1)
    tick(2)
    for k in (0, 1, 2):
        pair_tick(k)
    kernel_terms(1)
    tick(3)
    tick(4)
    relay(0)
    tick(5)
    for k in (3, 4, 5):
        pair_tick(k)
    kernel_terms(2)
    relay(1)
    tick(6)
    forward(0)
    tick(7)
    relay(2)
    tick(8)
    for k in (6, 7, 8):
        pair_tick(k)
    kernel_terms(3)
    relay(3)
    relay(4)
    relay(5)
    complete(0)
    for u in range(frames):
        convolve(u)
    out_ref[...] = jnp.transpose(frames_out[...], (1, 0, 2))
    forward(1)
    complete(1)

    for h in range(2):
        @pl.when(z > 0)
        def _():
            share_right(z, h, right_in).wait_recv()

        @pl.when(z < n - 1)
        def _():
            share_left(z, h, left_in).wait_recv()

    def slope_frame(s, _):
        wide = f_ref[s].astype(jnp.float32)
        logistic = jax.nn.sigmoid(wide)
        slope = logistic * (1.0 + wide * (1.0 - logistic))

        def keep(total):
            frames_out[s] = (total * slope).astype(jnp.bfloat16)

        own = part[z, s].astype(jnp.float32)

        @pl.when(z == 0)
        def _():
            keep(own + left_in[z, s].astype(jnp.float32))

        @pl.when(z == n - 1)
        def _():
            keep(own + right_in[z, s].astype(jnp.float32))

        @pl.when((z > 0) & (z < n - 1))
        def _():
            keep(own + (left_in[z, s].astype(jnp.float32) + right_in[z, s].astype(jnp.float32)))

        return 0

    lax.fori_loop(0, frames, slope_frame, 0)
    fg_ref[...] = jnp.transpose(frames_out[...], (1, 0, 2))
    forward(2)
    complete(2)

    for p in range(total_pieces):
        @pl.when((z < n - 1) & (p < (z + 1) * per))
        def _():
            pass_right(p).wait_send()

        @pl.when((z > 0) & (p >= z * per))
        def _():
            pass_left(p).wait_send()

        @pl.when((p < z * per) | (p >= (z + 1) * per))
        def _():
            pair_copy(p, t).wait_send()

    for h in range(2):
        for j in range(n - 1):
            @pl.when(z < n - 1 - j)
            def _():
                share_right(n - 1 - j, h, right_in).wait_send()

            @pl.when(z > j)
            def _():
                share_left(j, h, left_in).wait_send()

    own_copy(t).wait_send()
    cot_copy().wait_send()

    @pl.when(t == 1)
    def _():
        halo_copy().wait_send()

    for i in range(n - 1):
        for a in range(3):
            sum_copy(i, a).wait_send()
            keep_copy(i, a, t).wait_send()
            done_copy(i, a, t).wait_send()

    forward(n - 1)
    complete(n - 1)
    for a in range(3):
        sum_copy(n - 1, a).wait_send()
        keep_copy(n - 1, a, t).wait_send()
        done_copy(n - 1, a, t).wait_send()


def write(out_ref, fg_ref, kg_ref, out_hbm, fg_hbm, kg_hbm, sems):
    copies = [
        pltpu.make_async_copy(kg_ref, kg_hbm, sems.at[0]),
        pltpu.make_async_copy(out_ref, out_hbm, sems.at[1]),
        pltpu.make_async_copy(fg_ref, fg_hbm, sems.at[2]),
    ]
    for copy in copies:
        copy.start()
    for copy in copies:
        copy.wait()


LANES = 128


def fits(mesh, features, kernel):
    c, clips, frames, pixels = features.shape
    return (
        mesh.shape["tm"] == 2
        and mesh.shape["chan"] == 4
        and mesh.shape["dp"] == 2
        and clips == 1
        and frames == 4
        and c * mesh.shape["chan"] == kernel.shape[2]
        and kernel.shape[2] == 3 * LANES
        and pixels % 128 == 0
        and pixels % WID == 0
        and kernel.size * 24 + features.size * 96 < 56 * 2**20
    )


def fused(mesh, features, kernel, cotangent):
    c, clips, frames, pixels = features.shape
    n = mesh.shape["chan"]
    full = c * n
    scale = 1.0 / math.sqrt(mesh.shape["dp"] * mesh.shape["tm"] * clips * frames * pixels)
    vmem = pl.BlockSpec(memory_space=pltpu.VMEM)
    hbm = pl.BlockSpec(memory_space=pltpu.HBM)
    b16, f32 = jnp.bfloat16, jnp.float32
    dma = pltpu.SemaphoreType.DMA
    half = c // 2
    rows = math.gcd(c, LANES)
    pieces = full // rows
    sums = 3 * n
    spare = LANES - c
    kept = 9 - 9 // (c // spare + 1)
    limit = 8 * 2**20 + kernel.size * 22 + features.size * 64
    in_hbm = lambda x: pltpu.with_memory_space_constraint(x, pltpu.HBM)
    shards = pltpu.VMEM((n, frames, c, pixels), b16)
    by_frame = pltpu.VMEM((frames, c, pixels), b16)
    by_channel = pltpu.VMEM((c, frames, pixels), b16)
    halves = pltpu.VMEM((n, 2, 3 * kept, half, LANES), b16)
    shapes = (
        jax.ShapeDtypeStruct((c, frames, pixels), b16),
        jax.ShapeDtypeStruct((c, frames, pixels), b16),
        jax.ShapeDtypeStruct((27, c, full), f32),
    )
    held = pl.pallas_call(
        functools.partial(body, (n, LANES, rows, scale)),
        out_shape=shapes,
        in_specs=[hbm, hbm, hbm],
        out_specs=(vmem,) * 3,
        scratch_shapes=[
            by_channel, by_channel, by_frame, by_frame,
            pltpu.VMEM((27, c, full), b16),
            pltpu.VMEM((9, c, (2 * frames + 2) * pixels), b16),
            pltpu.VMEM((full, 27 * c), b16),
            pltpu.VMEM((full, (2 * frames + 2) * pixels), b16),
            by_frame,
            shards, shards, shards,
            pltpu.VMEM((9, c, pixels), f32),
            by_frame,
            halves, halves,
            dma, dma, dma, dma((pieces,)), dma((pieces,)), dma((pieces,)), dma((pieces,)), dma((pieces,)), dma, dma,
            dma, dma, dma, dma, dma((2 * n,)), dma((2 * n,)), dma((2 * n,)), dma((2 * n,)),
            dma((sums,)), dma((sums,)), dma((sums,)), dma((sums,)), dma((sums,)), dma((sums,)),
        ],
        compiler_params=pltpu.CompilerParams(
            collective_id=0, has_side_effects=True, vmem_limit_bytes=limit
        ),
        name="video_conv",
    )(
        in_hbm(features.reshape(c, frames, pixels)),
        in_hbm(jnp.transpose(kernel, (1, 0, 2))),
        in_hbm(cotangent.reshape(c, frames, pixels)),
    )
    conv_out, feature_grad, kernel_grad = pl.pallas_call(
        write,
        out_shape=shapes,
        in_specs=[vmem] * 3,
        out_specs=(hbm,) * 3,
        scratch_shapes=[dma((3,))],
        compiler_params=pltpu.CompilerParams(vmem_limit_bytes=12 * 2**20),
        name="write",
    )(*held)
    return conv_out.reshape(features.shape), feature_grad.reshape(features.shape), jnp.transpose(kernel_grad, (1, 0, 2))


def solution(mesh):
    def chosen(features, kernel, cotangent):
        if fits(mesh, features, kernel):
            return fused(mesh, features, kernel, cotangent)
        return local(features, kernel, cotangent)

    return jax.shard_map(
        chosen,
        mesh=mesh,
        in_specs=(
            P("chan", ("groups", "dp"), "tm", None),
            P("chan", None, None),
            P("chan", ("groups", "dp"), "tm", None),
        ),
        out_specs=(
            P("chan", ("groups", "dp"), "tm", None),
            P("chan", ("groups", "dp"), "tm", None),
            P(("groups", "chan"), None, None),
        ),
        check_vma=False,
    )
```

```python
import functools
import math

import jax
import jax.numpy as jnp
from jax import lax
from jax.experimental import pallas as pl
from jax.experimental.pallas import tpu as pltpu
from jax.sharding import PartitionSpec as P

WID = 64


def from_behind(x, axis, by):
    size = lax.axis_size(axis)
    pairs = [(i, i + by) for i in range(size) if 0 <= i + by < size]
    return lax.ppermute(x, axis, pairs)


def padded_copies(block):
    pixels = block.shape[-1]
    column = lax.broadcasted_iota(jnp.int32, (pixels,), 0) % WID
    nothing = jnp.zeros((), block.dtype)
    widths = [(0, 0), (0, 0), (0, 0), (WID + 1, WID + 1)]
    left_cut = jnp.pad(jnp.where(column == WID - 1, nothing, block), widths)
    untouched = jnp.pad(block, widths)
    right_cut = jnp.pad(jnp.where(column == 0, nothing, block), widths)
    return (left_cut, untouched, right_cut)


def tap_window(copies, first_frame, vertical, horizontal, frames, pixels):
    source = copies[horizontal]
    offset = vertical * WID + horizontal
    return source[:, :, first_frame : first_frame + frames, offset : offset + pixels]


def stacked_taps(copies, first_frame, flipped, frames, pixels):
    pieces = []
    for vertical in range(3):
        for horizontal in range(3):
            if flipped:
                pieces.append(
                    tap_window(copies, first_frame, 2 - vertical, 2 - horizontal, frames, pixels)
                )
            else:
                pieces.append(tap_window(copies, first_frame, vertical, horizontal, frames, pixels))
    concatenated = jnp.concatenate(pieces, axis=0)
    return concatenated.reshape(concatenated.shape[0], -1)


def local(features, kernel, cotangent):
    channels, clip_count, frames, pixels = features.shape
    flat_length = clip_count * frames * pixels
    widened = features.astype(jnp.float32)
    logistic = jax.nn.sigmoid(widened)
    activation = (widened * logistic).astype(jnp.bfloat16)
    slope_factor = logistic * (1.0 + widened * (1.0 - logistic))
    earlier = from_behind(activation[:, :, frames - 2 :, :], "tm", 1)
    extended = jnp.concatenate([earlier, activation], axis=2)
    upcoming = from_behind(cotangent[:, :, :2, :], "tm", -1)
    later_padded = jnp.concatenate([cotangent, upcoming], axis=2)
    cotangent_rows = cotangent.reshape(channels, -1)
    portion = lax.all_gather(extended, "chan", axis=0, tiled=True)
    out_sum = jnp.zeros((channels, flat_length), jnp.float32)
    amount = portion.shape[0]
    copies = padded_copies(portion)
    kernel_cols = kernel
    grad_parts = []
    for forward_temporal in range(3):
        stacked = stacked_taps(copies, forward_temporal, False, frames, pixels)
        weights = kernel_cols[:, 9 * forward_temporal : 9 * forward_temporal + 9, :].reshape(
            channels, 9 * amount
        )
        out_sum = out_sum + jnp.dot(weights, stacked, preferred_element_type=jnp.float32)
        grad_parts.append(
            lax.dot_general(
                cotangent_rows,
                stacked,
                (((1,), (1,)), ((), ())),
                preferred_element_type=jnp.float32,
            ).reshape(channels, 9, amount)
        )
    grad_sum = jnp.concatenate(grad_parts, axis=1)
    out_sum, grad_sum = (out_sum, grad_sum)
    conv_out = out_sum.reshape(features.shape).astype(jnp.bfloat16)
    position_count = lax.axis_size("dp") * lax.axis_size("tm") * flat_length
    kernel_grad = lax.psum(grad_sum, ("tm", "dp")) * (1.0 / math.sqrt(position_count))
    padded_later = padded_copies(later_padded)
    later_stacks = [
        stacked_taps(padded_later, 2 - temporal, True, frames, pixels) for temporal in range(3)
    ]
    amount = channels * lax.axis_size("chan")
    kernel_cols = kernel
    summed = jnp.zeros((amount, flat_length), jnp.float32)
    for temporal in range(3):
        weights = jnp.transpose(
            kernel_cols[:, 9 * temporal : 9 * temporal + 9, :], (2, 1, 0)
        ).reshape(amount, 9 * channels)
        summed = summed + jnp.dot(
            weights, later_stacks[temporal], preferred_element_type=jnp.float32
        )
    before_slope = lax.psum_scatter(
        summed.reshape(amount, clip_count, frames, pixels), "chan", scatter_dimension=0, tiled=True
    )
    feature_grad = (before_slope * slope_factor).astype(jnp.bfloat16)
    return (conv_out, feature_grad, kernel_grad)


def moved(x, rows, columns, pixels):
    step = rows * WID + columns
    place = lax.broadcasted_iota(jnp.int32, (1, pixels), 1)
    row, column = place // WID + rows, place % WID + columns
    out = x if step == 0 else pltpu.roll(x, (-step) % pixels, len(x.shape) - 1)
    inside = None
    if rows:
        inside = (row >= 0) & (row < pixels // WID)
    if columns:
        within = (column >= 0) & (column < WID)
        inside = within if inside is None else inside & within
    return out if inside is None else out * jnp.where(inside, 1.0, 0.0)


def silu(x):
    wide = x.astype(jnp.float32)
    return wide * jax.nn.sigmoid(wide)


def body(
    sizes,
    f_hbm, w_hbm, g_hbm,
    out_ref, fg_ref, kg_ref,
    f_raw, g_raw, f_ref, g_ref, w_ref, stack, turned, act, cot_in, part, right_in, left_in, taps, frames_out, mine, theirs,
    f_sem, g_sem, w_sem, gather_right, gather_left, gather_recv, pair_send, pair_recv, own_send, own_recv,
    cot_send, cot_recv, halo_send, halo_recv, right_send, right_recv, left_send, left_recv,
    sum_send, sum_recv, keep_send, keep_recv, done_send, done_recv,
):
    n, lanes, rows, scale = sizes
    c, frames, pixels = f_raw.shape
    full = c * n
    half = c // 2
    long = frames * pixels
    every = 2 * frames
    per = c // rows
    total_pieces = per * n
    spare = lanes - c
    thirds = c // spare
    extra = 9 // (thirds + 1)
    kept = 9 - extra
    z, t, d = lax.axis_index("chan"), lax.axis_index("tm"), lax.axis_index("dp")

    def remote(src, dst, send, recv, **where):
        return pltpu.make_async_remote_copy(
            src_ref=src, dst_ref=dst, send_sem=send, recv_sem=recv,
            device_id=where, device_id_type=pl.DeviceIdType.MESH,
        )

    barrier = pltpu.get_barrier_semaphore()

    def greet(**where):
        pl.semaphore_signal(barrier, inc=1, device_id=where, device_id_type=pl.DeviceIdType.MESH)

    greet(dp=1 - d)

    @pl.when(z < n - 1)
    def _():
        greet(chan=z + 1)

    @pl.when(z > 0)
    def _():
        greet(chan=z - 1)

    greet(tm=1 - t)
    load_f = pltpu.make_async_copy(f_hbm, f_raw, f_sem)
    load_g = pltpu.make_async_copy(g_hbm, g_raw, g_sem)
    load_w = pltpu.make_async_copy(w_hbm, w_ref, w_sem)
    load_g.start()
    load_f.start()
    load_w.start()

    def half_rows(which):
        return pl.ds(pl.multiple_of(which * half, half), half)

    def frame_lanes(s):
        return pl.ds(pl.multiple_of(s * pixels, pixels), pixels)

    def own_lanes(which):
        return pl.ds(pl.multiple_of((which * frames + 2) * pixels, pixels), long)

    def shard_rows(q):
        return pl.ds(pl.multiple_of(q * c, c), c)

    def piece(p, which):
        return act.at[pl.ds(pl.multiple_of(p * rows, rows), rows), own_lanes(which)]

    def stack_frame(x, s, at):
        wide = x.astype(jnp.float32)
        for i in range(3):
            for j in range(3):
                stack[3 * i + j, at, frame_lanes(s)] = moved(wide, 1 - i, 1 - j, pixels).astype(jnp.bfloat16)

    everything = pl.ds(0, c)

    def own_frame(s, _):
        stack_frame(g_ref[s], t * frames + s, everything)
        return 0

    act[:, 0 : 2 * pixels] = jnp.zeros((full, 2 * pixels), jnp.bfloat16)
    stack[:, :, every * pixels : (every + 2) * pixels] = jnp.zeros((9, c, 2 * pixels), jnp.bfloat16)
    load_g.wait()
    g_ref[...] = jnp.transpose(g_raw[...], (1, 0, 2))
    load_f.wait()
    f_ref[...] = jnp.transpose(f_raw[...], (1, 0, 2))
    for s in range(frames):
        act[shard_rows(z), frame_lanes(t * frames + s + 2)] = silu(f_ref[s]).astype(jnp.bfloat16)
    lax.fori_loop(0, frames, own_frame, 0)

    @pl.when((z > 0) & (z < n - 1))
    def _():
        pl.semaphore_wait(barrier, 4)

    @pl.when((z == 0) | (z == n - 1))
    def _():
        pl.semaphore_wait(barrier, 3)

    def pass_right(p):
        return remote(piece(p, t), piece(p, t), gather_right.at[p], gather_recv.at[p], chan=z + 1)

    def pass_left(p):
        return remote(piece(p, t), piece(p, t), gather_left.at[p], gather_recv.at[p], chan=z - 1)

    def pair_copy(p, which):
        return remote(piece(p, which), piece(p, which), pair_send.at[p], pair_recv.at[p], tm=1 - t)

    def own_copy(which):
        place = act.at[shard_rows(z), own_lanes(which)]
        return remote(place, place, own_send, own_recv, tm=1 - t)

    def cot_copy():
        return remote(
            g_ref.at[:, half_rows(1 - t)], cot_in.at[:, half_rows(1 - t)], cot_send, cot_recv, tm=1 - t
        )

    def halo_copy():
        return remote(
            g_ref.at[pl.ds(0, 2), half_rows(1)], cot_in.at[pl.ds(0, 2), half_rows(1)], halo_send, halo_recv, tm=1 - t
        )

    cot_copy().start()
    own_copy(t).start()

    @pl.when(t == 1)
    def _():
        halo_copy().start()

    for k in range(per):
        @pl.when(z < n - 1)
        def _():
            pass_right(z * per + per - 1 - k).start()

        @pl.when(z > 0)
        def _():
            pass_left(z * per + k).start()

    def other_frame(s, _):
        stack_frame(cot_in[s, half_rows(t), :], (1 - t) * frames + s, half_rows(t))
        return 0

    def tick(k):
        @pl.when((z + 1) * per + k < total_pieces)
        def _():
            p = (z + 1) * per + k
            pass_left(p).wait_recv()

            @pl.when(z > 0)
            def _():
                pass_left(p).start()

            pair_copy(p, t).start()

        @pl.when(z * per - 1 - k >= 0)
        def _():
            p = z * per - 1 - k
            pass_right(p).wait_recv()

            @pl.when(z < n - 1)
            def _():
                pass_right(p).start()

            pair_copy(p, t).start()

    def pair_tick(k):
        @pl.when((z + 1) * per + k < total_pieces)
        def _():
            pair_copy((z + 1) * per + k, 1 - t).wait_recv()

        @pl.when(z * per - 1 - k >= 0)
        def _():
            pair_copy(z * per - 1 - k, 1 - t).wait_recv()

    def shard_of(i):
        near, far = z + 1 - 2 * (z // 2), (n - 1) - (n - 1) * (z // 2)
        return (z, near, 2 * (n - 1) - z - near - far, far)[i]

    def cell(ref, i, a, which):
        return ref.at[i, which, pl.ds(kept * a, kept)]

    def sum_copy(i, a):
        return remote(
            cell(mine, i, a, t), cell(theirs, i, a, t), sum_send.at[3 * i + a], sum_recv.at[3 * i + a], dp=1 - d
        )

    def keep_copy(i, which):
        place = mine.at[i, which]
        return remote(place, place, keep_send.at[i], keep_recv.at[i], tm=1 - t)

    def done_copy(i, a, which):
        place = cell(theirs, i, a, which)
        return remote(place, place, done_send.at[3 * i + a], done_recv.at[3 * i + a], tm=1 - t)

    def lane_of(shape):
        return lax.broadcasted_iota(jnp.int32, shape, len(shape) - 1)

    def matched(held, channels):
        cut = held.shape[0] // 32 * 16
        return jnp.concatenate(
            [
                lax.dot_general(x, channels, (((1,), (1,)), ((), ())), preferred_element_type=jnp.float32)
                for x in (held[:cut], held[cut:])
            ],
            axis=0,
        )

    def send_terms(i, a, terms):
        last = terms[kept * half :]
        for h in range(thirds):
            block = terms[h * extra * half : (h + 1) * extra * half]
            block = jnp.where(lane_of(block.shape) < c, block, pltpu.roll(last, c - spare * h, 1))
            mine[i, t, kept * a + h * extra : kept * a + (h + 1) * extra] = block.reshape(
                extra, half, lanes
            ).astype(jnp.bfloat16)
        mine[i, t, kept * a + thirds * extra : kept * (a + 1)] = terms[thirds * extra * half : kept * half].reshape(
            kept - thirds * extra, half, lanes
        ).astype(jnp.bfloat16)
        sum_copy(i, a).start()

    def kernel_terms(i):
        at = shard_rows(shard_of(i))

        def channels(first, count):
            return [
                act[at, first * pixels : (first + count) * pixels],
                jnp.zeros((spare, count * pixels), jnp.bfloat16),
            ]

        def held(first):
            return stack[:, half_rows(t), first * pixels : every * pixels].reshape(9 * half, (every - first) * pixels)

        pair = matched(held(0), jnp.concatenate(channels(1, every) + channels(2, every), axis=0))
        send_terms(i, 1, pair[:, :lanes])
        send_terms(i, 2, pair[:, lanes:])
        send_terms(i, 0, matched(held(2), jnp.concatenate(channels(2, every - 2), axis=0)))
        keep_copy(i, t).start()

    def assemble(i, a, which):
        at = shard_of(i) * c
        both = (
            mine[i, which, kept * a : kept * (a + 1)].astype(jnp.float32)
            + theirs[i, which, kept * a : kept * (a + 1)].astype(jnp.float32)
        ) * scale
        last = None
        for h in reversed(range(thirds)):
            block = pltpu.roll(both[h * extra : (h + 1) * extra].reshape(extra * half, lanes), spare * (h + 1), 1)
            last = block if last is None else jnp.where(lane_of(block.shape) < spare * (h + 1), block, last)
        whole = jnp.concatenate([both.reshape(kept * half, lanes), last], axis=0)
        start = at % lanes
        turned_lanes = pltpu.roll(whole, start, 1).reshape(9, half, lanes)
        lane = lane_of(turned_lanes.shape)
        tile = at // lanes

        def put(tile, inside):
            place = (pl.ds(9 * a, 9), half_rows(which), pl.ds(pl.multiple_of(tile * lanes, lanes), lanes))
            kg_ref[place] = jnp.where(inside, turned_lanes, kg_ref[place])

        put(tile, (lane >= start) & (lane < start + c))

        @pl.when(start + c > lanes)
        def _():
            put(tile + 1, lane < start + c - lanes)

    def before(s):
        rhs = jnp.concatenate(
            [stack[:, :, frame_lanes(t * frames + s + 2 - a)].reshape(9 * c, pixels) for a in range(3)], axis=0
        )
        total = jnp.dot(turned[...], rhs, preferred_element_type=jnp.float32)
        for q in range(n):
            part[q, s] = total[q * c : (q + 1) * c].astype(jnp.bfloat16)

    few = frames // 2

    def share_right(q, h, src):
        at = pl.ds(h * few, few)
        return remote(src.at[q, at], right_in.at[q, at], right_send.at[2 * q + h], right_recv.at[2 * q + h], chan=z + 1)

    def share_left(q, h, src):
        at = pl.ds(h * few, few)
        return remote(src.at[q, at], left_in.at[q, at], left_send.at[2 * q + h], left_recv.at[2 * q + h], chan=z - 1)

    def first_share(j, h):
        @pl.when(z == 0)
        def _():
            share_right(n - 1 - j, h, part).start()

        @pl.when(z == n - 1)
        def _():
            share_left(j, h, part).start()

    def add_part(held, q, h):
        for s in range(h * few, (h + 1) * few):
            held[q, s] = (held[q, s].astype(jnp.float32) + part[q, s].astype(jnp.float32)).astype(jnp.bfloat16)

    def relay_right(q, h):
        share_right(q, h, right_in).wait_recv()
        add_part(right_in, q, h)
        share_right(q, h, right_in).start()

    def relay_left(q, h):
        share_left(q, h, left_in).wait_recv()
        add_part(left_in, q, h)
        share_left(q, h, left_in).start()

    def relay(k):
        kind, h = ((0, 0), (0, 1), (2, 0), (1, 0), (2, 1), (1, 1))[k]

        @pl.when(z == 1)
        def _():
            if kind == 2:
                relay_left(0, h)
            else:
                relay_right(n - 1 - kind, h)

        @pl.when(z == 2)
        def _():
            if kind == 2:
                relay_right(n - 1, h)
            else:
                relay_left(kind, h)

    def convolve(u):
        rhs = jnp.concatenate([act[:, frame_lanes(t * frames + u + a)] for a in range(3)], axis=0)
        lhs = jnp.concatenate([w_ref[9 * a : 9 * a + 9].reshape(9 * c, full) for a in range(3)], axis=1)
        taps[...] = jnp.dot(lhs, rhs, preferred_element_type=jnp.float32).reshape(9, c, pixels)
        result = jnp.zeros((c, pixels), jnp.float32)
        for i in range(3):
            for j in range(3):
                result = result + moved(taps[3 * i + j], i - 1, j - 1, pixels)
        frames_out[u] = result.astype(jnp.bfloat16)

    def forward(i):
        for a in (1, 2, 0):
            sum_copy(i, a).wait_recv()
            done_copy(i, a, t).start()
            assemble(i, a, t)

    def complete(i):
        keep_copy(i, 1 - t).wait_recv()
        for a in (1, 2, 0):
            done_copy(i, a, 1 - t).wait_recv()
            assemble(i, a, 1 - t)

    cot_copy().wait_recv()
    lax.fori_loop(0, frames, other_frame, 0)
    own_copy(1 - t).wait_recv()
    kernel_terms(0)

    @pl.when(t == 0)
    def _():
        halo_copy().wait_recv()

        def next_frame(s, _):
            stack_frame(cot_in[s, half_rows(1), :], frames + s, half_rows(1))
            return 0

        lax.fori_loop(0, 2, next_frame, 0)

    load_w.wait()
    turned[...] = jnp.transpose(w_ref[...].reshape(27 * c, full))
    before(0)
    before(1)
    first_share(0, 0)
    tick(0)
    before(2)
    before(3)
    first_share(0, 1)
    for j in range(1, n - 1):
        for h in range(2):
            first_share(j, h)
    tick(1)
    tick(2)
    for k in (0, 1, 2):
        pair_tick(k)
    kernel_terms(1)
    tick(3)
    tick(4)
    tick(5)
    for k in (3, 4, 5):
        pair_tick(k)
    kernel_terms(2)
    relay(0)
    relay(1)
    tick(6)
    tick(7)
    tick(8)
    for k in (6, 7, 8):
        pair_tick(k)
    kernel_terms(3)
    forward(0)
    relay(2)
    relay(3)
    relay(4)
    relay(5)
    complete(0)
    for u in range(frames):
        convolve(u)
    out_ref[...] = jnp.transpose(frames_out[...], (1, 0, 2))
    forward(1)
    complete(1)

    for h in range(2):
        @pl.when(z > 0)
        def _():
            share_right(z, h, right_in).wait_recv()

        @pl.when(z < n - 1)
        def _():
            share_left(z, h, left_in).wait_recv()

    def slope_frame(s, _):
        wide = f_ref[s].astype(jnp.float32)
        logistic = jax.nn.sigmoid(wide)
        slope = logistic * (1.0 + wide * (1.0 - logistic))

        def keep(total):
            frames_out[s] = (total * slope).astype(jnp.bfloat16)

        own = part[z, s].astype(jnp.float32)

        @pl.when(z == 0)
        def _():
            keep(own + left_in[z, s].astype(jnp.float32))

        @pl.when(z == n - 1)
        def _():
            keep(own + right_in[z, s].astype(jnp.float32))

        @pl.when((z > 0) & (z < n - 1))
        def _():
            keep(own + (left_in[z, s].astype(jnp.float32) + right_in[z, s].astype(jnp.float32)))

        return 0

    lax.fori_loop(0, frames, slope_frame, 0)
    fg_ref[...] = jnp.transpose(frames_out[...], (1, 0, 2))
    forward(2)
    complete(2)

    for p in range(total_pieces):
        @pl.when((z < n - 1) & (p < (z + 1) * per))
        def _():
            pass_right(p).wait_send()

        @pl.when((z > 0) & (p >= z * per))
        def _():
            pass_left(p).wait_send()

        @pl.when((p < z * per) | (p >= (z + 1) * per))
        def _():
            pair_copy(p, t).wait_send()

    for h in range(2):
        for j in range(n - 1):
            @pl.when(z < n - 1 - j)
            def _():
                share_right(n - 1 - j, h, right_in).wait_send()

            @pl.when(z > j)
            def _():
                share_left(j, h, left_in).wait_send()

    own_copy(t).wait_send()
    cot_copy().wait_send()

    @pl.when(t == 1)
    def _():
        halo_copy().wait_send()

    for i in range(n - 1):
        keep_copy(i, t).wait_send()
        for a in range(3):
            sum_copy(i, a).wait_send()
            done_copy(i, a, t).wait_send()

    forward(n - 1)
    complete(n - 1)
    keep_copy(n - 1, t).wait_send()
    for a in range(3):
        sum_copy(n - 1, a).wait_send()
        done_copy(n - 1, a, t).wait_send()


def write(out_ref, fg_ref, kg_ref, out_hbm, fg_hbm, kg_hbm, sems):
    copies = [
        pltpu.make_async_copy(kg_ref, kg_hbm, sems.at[0]),
        pltpu.make_async_copy(out_ref, out_hbm, sems.at[1]),
        pltpu.make_async_copy(fg_ref, fg_hbm, sems.at[2]),
    ]
    for copy in copies:
        copy.start()
    for copy in copies:
        copy.wait()


LANES = 128


def fits(mesh, features, kernel):
    c, clips, frames, pixels = features.shape
    return (
        mesh.shape["tm"] == 2
        and mesh.shape["chan"] == 4
        and mesh.shape["dp"] == 2
        and clips == 1
        and frames == 4
        and c * mesh.shape["chan"] == kernel.shape[2]
        and kernel.shape[2] == 3 * LANES
        and pixels % 128 == 0
        and pixels % WID == 0
        and kernel.size * 24 + features.size * 96 < 56 * 2**20
    )


def fused(mesh, features, kernel, cotangent):
    c, clips, frames, pixels = features.shape
    n = mesh.shape["chan"]
    full = c * n
    scale = 1.0 / math.sqrt(mesh.shape["dp"] * mesh.shape["tm"] * clips * frames * pixels)
    vmem = pl.BlockSpec(memory_space=pltpu.VMEM)
    hbm = pl.BlockSpec(memory_space=pltpu.HBM)
    b16, f32 = jnp.bfloat16, jnp.float32
    dma = pltpu.SemaphoreType.DMA
    half = c // 2
    rows = math.gcd(c, LANES)
    pieces = full // rows
    sums = 3 * n
    spare = LANES - c
    kept = 9 - 9 // (c // spare + 1)
    limit = 8 * 2**20 + kernel.size * 22 + features.size * 64
    in_hbm = lambda x: pltpu.with_memory_space_constraint(x, pltpu.HBM)
    shards = pltpu.VMEM((n, frames, c, pixels), b16)
    by_frame = pltpu.VMEM((frames, c, pixels), b16)
    by_channel = pltpu.VMEM((c, frames, pixels), b16)
    halves = pltpu.VMEM((n, 2, 3 * kept, half, LANES), b16)
    shapes = (
        jax.ShapeDtypeStruct((c, frames, pixels), b16),
        jax.ShapeDtypeStruct((c, frames, pixels), b16),
        jax.ShapeDtypeStruct((27, c, full), f32),
    )
    held = pl.pallas_call(
        functools.partial(body, (n, LANES, rows, scale)),
        out_shape=shapes,
        in_specs=[hbm, hbm, hbm],
        out_specs=(vmem,) * 3,
        scratch_shapes=[
            by_channel, by_channel, by_frame, by_frame,
            pltpu.VMEM((27, c, full), b16),
            pltpu.VMEM((9, c, (2 * frames + 2) * pixels), b16),
            pltpu.VMEM((full, 27 * c), b16),
            pltpu.VMEM((full, (2 * frames + 2) * pixels), b16),
            by_frame,
            shards, shards, shards,
            pltpu.VMEM((9, c, pixels), f32),
            by_frame,
            halves, halves,
            dma, dma, dma, dma((pieces,)), dma((pieces,)), dma((pieces,)), dma((pieces,)), dma((pieces,)), dma, dma,
            dma, dma, dma, dma, dma((2 * n,)), dma((2 * n,)), dma((2 * n,)), dma((2 * n,)),
            dma((sums,)), dma((sums,)), dma((sums,)), dma((sums,)), dma((sums,)), dma((sums,)),
        ],
        compiler_params=pltpu.CompilerParams(
            collective_id=0, has_side_effects=True, vmem_limit_bytes=limit
        ),
        name="video_conv",
    )(
        in_hbm(features.reshape(c, frames, pixels)),
        in_hbm(jnp.transpose(kernel, (1, 0, 2))),
        in_hbm(cotangent.reshape(c, frames, pixels)),
    )
    conv_out, feature_grad, kernel_grad = pl.pallas_call(
        write,
        out_shape=shapes,
        in_specs=[vmem] * 3,
        out_specs=(hbm,) * 3,
        scratch_shapes=[dma((3,))],
        compiler_params=pltpu.CompilerParams(vmem_limit_bytes=12 * 2**20),
        name="write",
    )(*held)
    return conv_out.reshape(features.shape), feature_grad.reshape(features.shape), jnp.transpose(kernel_grad, (1, 0, 2))


def solution(mesh):
    def chosen(features, kernel, cotangent):
        if fits(mesh, features, kernel):
            return fused(mesh, features, kernel, cotangent)
        return local(features, kernel, cotangent)

    return jax.shard_map(
        chosen,
        mesh=mesh,
        in_specs=(
            P("chan", ("groups", "dp"), "tm", None),
            P("chan", None, None),
            P("chan", ("groups", "dp"), "tm", None),
        ),
        out_specs=(
            P("chan", ("groups", "dp"), "tm", None),
            P("chan", ("groups", "dp"), "tm", None),
            P(("groups", "chan"), None, None),
        ),
        check_vma=False,
    )
```

```python
import functools
import math

import jax
import jax.numpy as jnp
from jax import lax
from jax.experimental import pallas as pl
from jax.experimental.pallas import tpu as pltpu
from jax.sharding import PartitionSpec as P

WID = 64


def from_behind(x, axis, by):
    size = lax.axis_size(axis)
    pairs = [(i, i + by) for i in range(size) if 0 <= i + by < size]
    return lax.ppermute(x, axis, pairs)


def padded_copies(block):
    pixels = block.shape[-1]
    column = lax.broadcasted_iota(jnp.int32, (pixels,), 0) % WID
    nothing = jnp.zeros((), block.dtype)
    widths = [(0, 0), (0, 0), (0, 0), (WID + 1, WID + 1)]
    left_cut = jnp.pad(jnp.where(column == WID - 1, nothing, block), widths)
    untouched = jnp.pad(block, widths)
    right_cut = jnp.pad(jnp.where(column == 0, nothing, block), widths)
    return (left_cut, untouched, right_cut)


def tap_window(copies, first_frame, vertical, horizontal, frames, pixels):
    source = copies[horizontal]
    offset = vertical * WID + horizontal
    return source[:, :, first_frame : first_frame + frames, offset : offset + pixels]


def stacked_taps(copies, first_frame, flipped, frames, pixels):
    pieces = []
    for vertical in range(3):
        for horizontal in range(3):
            if flipped:
                pieces.append(
                    tap_window(copies, first_frame, 2 - vertical, 2 - horizontal, frames, pixels)
                )
            else:
                pieces.append(tap_window(copies, first_frame, vertical, horizontal, frames, pixels))
    concatenated = jnp.concatenate(pieces, axis=0)
    return concatenated.reshape(concatenated.shape[0], -1)


def local(features, kernel, cotangent):
    channels, clip_count, frames, pixels = features.shape
    flat_length = clip_count * frames * pixels
    widened = features.astype(jnp.float32)
    logistic = jax.nn.sigmoid(widened)
    activation = (widened * logistic).astype(jnp.bfloat16)
    slope_factor = logistic * (1.0 + widened * (1.0 - logistic))
    earlier = from_behind(activation[:, :, frames - 2 :, :], "tm", 1)
    extended = jnp.concatenate([earlier, activation], axis=2)
    upcoming = from_behind(cotangent[:, :, :2, :], "tm", -1)
    later_padded = jnp.concatenate([cotangent, upcoming], axis=2)
    cotangent_rows = cotangent.reshape(channels, -1)
    portion = lax.all_gather(extended, "chan", axis=0, tiled=True)
    out_sum = jnp.zeros((channels, flat_length), jnp.float32)
    amount = portion.shape[0]
    copies = padded_copies(portion)
    kernel_cols = kernel
    grad_parts = []
    for forward_temporal in range(3):
        stacked = stacked_taps(copies, forward_temporal, False, frames, pixels)
        weights = kernel_cols[:, 9 * forward_temporal : 9 * forward_temporal + 9, :].reshape(
            channels, 9 * amount
        )
        out_sum = out_sum + jnp.dot(weights, stacked, preferred_element_type=jnp.float32)
        grad_parts.append(
            lax.dot_general(
                cotangent_rows,
                stacked,
                (((1,), (1,)), ((), ())),
                preferred_element_type=jnp.float32,
            ).reshape(channels, 9, amount)
        )
    grad_sum = jnp.concatenate(grad_parts, axis=1)
    out_sum, grad_sum = (out_sum, grad_sum)
    conv_out = out_sum.reshape(features.shape).astype(jnp.bfloat16)
    position_count = lax.axis_size("dp") * lax.axis_size("tm") * flat_length
    kernel_grad = lax.psum(grad_sum, ("tm", "dp")) * (1.0 / math.sqrt(position_count))
    padded_later = padded_copies(later_padded)
    later_stacks = [
        stacked_taps(padded_later, 2 - temporal, True, frames, pixels) for temporal in range(3)
    ]
    amount = channels * lax.axis_size("chan")
    kernel_cols = kernel
    summed = jnp.zeros((amount, flat_length), jnp.float32)
    for temporal in range(3):
        weights = jnp.transpose(
            kernel_cols[:, 9 * temporal : 9 * temporal + 9, :], (2, 1, 0)
        ).reshape(amount, 9 * channels)
        summed = summed + jnp.dot(
            weights, later_stacks[temporal], preferred_element_type=jnp.float32
        )
    before_slope = lax.psum_scatter(
        summed.reshape(amount, clip_count, frames, pixels), "chan", scatter_dimension=0, tiled=True
    )
    feature_grad = (before_slope * slope_factor).astype(jnp.bfloat16)
    return (conv_out, feature_grad, kernel_grad)


def moved(x, rows, columns, pixels):
    step = rows * WID + columns
    place = lax.broadcasted_iota(jnp.int32, (1, pixels), 1)
    row, column = place // WID + rows, place % WID + columns
    out = x if step == 0 else pltpu.roll(x, (-step) % pixels, len(x.shape) - 1)
    inside = None
    if rows:
        inside = (row >= 0) & (row < pixels // WID)
    if columns:
        within = (column >= 0) & (column < WID)
        inside = within if inside is None else inside & within
    return out if inside is None else out * jnp.where(inside, 1.0, 0.0)


def silu(x):
    wide = x.astype(jnp.float32)
    return wide * jax.nn.sigmoid(wide)


def body(
    sizes,
    f_hbm, w_hbm, g_hbm,
    out_ref, fg_ref, kg_ref,
    f_raw, g_raw, f_ref, g_ref, w_ref, stack, turned, act, cot_in, part, right_in, left_in, taps, frames_out, mine, theirs,
    f_sem, g_sem, w_sem, gather_right, gather_left, gather_recv, pair_send, pair_recv, own_send, own_recv,
    cot_send, cot_recv, halo_send, halo_recv, right_send, right_recv, left_send, left_recv,
    sum_send, sum_recv, keep_send, keep_recv, done_send, done_recv, end_send, end_recv, far_send, far_recv,
):
    n, lanes, rows, scale = sizes
    c, frames, pixels = f_raw.shape
    full = c * n
    half = c // 2
    long = frames * pixels
    every = 2 * frames
    per = c // rows
    total_pieces = per * n
    spare = lanes - c
    thirds = c // spare
    extra = 9 // (thirds + 1)
    kept = 9 - extra
    z, t, d = lax.axis_index("chan"), lax.axis_index("tm"), lax.axis_index("dp")

    def remote(src, dst, send, recv, **where):
        return pltpu.make_async_remote_copy(
            src_ref=src, dst_ref=dst, send_sem=send, recv_sem=recv,
            device_id=where, device_id_type=pl.DeviceIdType.MESH,
        )

    barrier = pltpu.get_barrier_semaphore()

    def greet(**where):
        pl.semaphore_signal(barrier, inc=1, device_id=where, device_id_type=pl.DeviceIdType.MESH)

    greet(dp=1 - d)
    greet(dp=1 - d, tm=1 - t)

    @pl.when(z < n - 1)
    def _():
        greet(chan=z + 1)

    @pl.when(z > 0)
    def _():
        greet(chan=z - 1)

    greet(tm=1 - t)
    load_f = pltpu.make_async_copy(f_hbm, f_raw, f_sem)
    load_g = pltpu.make_async_copy(g_hbm, g_raw, g_sem)
    load_w = pltpu.make_async_copy(w_hbm, w_ref, w_sem)
    load_g.start()
    load_f.start()
    load_w.start()

    def half_rows(which):
        return pl.ds(pl.multiple_of(which * half, half), half)

    def frame_lanes(s):
        return pl.ds(pl.multiple_of(s * pixels, pixels), pixels)

    def own_lanes(which):
        return pl.ds(pl.multiple_of((which * frames + 2) * pixels, pixels), long)

    def shard_rows(q):
        return pl.ds(pl.multiple_of(q * c, c), c)

    def piece(p, which):
        return act.at[pl.ds(pl.multiple_of(p * rows, rows), rows), own_lanes(which)]

    def stack_frame(x, s, at):
        wide = x.astype(jnp.float32)
        for i in range(3):
            for j in range(3):
                stack[3 * i + j, at, frame_lanes(s)] = moved(wide, 1 - i, 1 - j, pixels).astype(jnp.bfloat16)

    everything = pl.ds(0, c)

    def own_frame(s, _):
        stack_frame(g_ref[s], t * frames + s, everything)
        return 0

    act[:, 0 : 2 * pixels] = jnp.zeros((full, 2 * pixels), jnp.bfloat16)
    stack[:, :, every * pixels : (every + 2) * pixels] = jnp.zeros((9, c, 2 * pixels), jnp.bfloat16)
    load_g.wait()
    g_ref[...] = jnp.transpose(g_raw[...], (1, 0, 2))
    load_f.wait()
    f_ref[...] = jnp.transpose(f_raw[...], (1, 0, 2))
    for s in range(frames):
        act[shard_rows(z), frame_lanes(t * frames + s + 2)] = silu(f_ref[s]).astype(jnp.bfloat16)
    lax.fori_loop(0, frames, own_frame, 0)

    @pl.when((z > 0) & (z < n - 1))
    def _():
        pl.semaphore_wait(barrier, 5)

    @pl.when((z == 0) | (z == n - 1))
    def _():
        pl.semaphore_wait(barrier, 4)

    def pass_right(p):
        return remote(piece(p, t), piece(p, t), gather_right.at[p], gather_recv.at[p], chan=z + 1)

    def pass_left(p):
        return remote(piece(p, t), piece(p, t), gather_left.at[p], gather_recv.at[p], chan=z - 1)

    def pair_copy(p, which):
        return remote(piece(p, which), piece(p, which), pair_send.at[p], pair_recv.at[p], tm=1 - t)

    def own_copy(which):
        place = act.at[shard_rows(z), own_lanes(which)]
        return remote(place, place, own_send, own_recv, tm=1 - t)

    def cot_copy():
        return remote(
            g_ref.at[:, half_rows(1 - t)], cot_in.at[:, half_rows(1 - t)], cot_send, cot_recv, tm=1 - t
        )

    def halo_copy():
        return remote(
            g_ref.at[pl.ds(0, 2), half_rows(1)], cot_in.at[pl.ds(0, 2), half_rows(1)], halo_send, halo_recv, tm=1 - t
        )

    cot_copy().start()
    own_copy(t).start()

    @pl.when(t == 1)
    def _():
        halo_copy().start()

    for k in range(per):
        @pl.when(z < n - 1)
        def _():
            pass_right(z * per + per - 1 - k).start()

        @pl.when(z > 0)
        def _():
            pass_left(z * per + k).start()

    def other_frame(s, _):
        stack_frame(cot_in[s, half_rows(t), :], (1 - t) * frames + s, half_rows(t))
        return 0

    def tick(k):
        @pl.when((z + 1) * per + k < total_pieces)
        def _():
            p = (z + 1) * per + k
            pass_left(p).wait_recv()

            @pl.when(z > 0)
            def _():
                pass_left(p).start()

            pair_copy(p, t).start()

        @pl.when(z * per - 1 - k >= 0)
        def _():
            p = z * per - 1 - k
            pass_right(p).wait_recv()

            @pl.when(z < n - 1)
            def _():
                pass_right(p).start()

            pair_copy(p, t).start()

    def pair_tick(k):
        @pl.when((z + 1) * per + k < total_pieces)
        def _():
            pair_copy((z + 1) * per + k, 1 - t).wait_recv()

        @pl.when(z * per - 1 - k >= 0)
        def _():
            pair_copy(z * per - 1 - k, 1 - t).wait_recv()

    def shard_of(i):
        near, far = z + 1 - 2 * (z // 2), (n - 1) - (n - 1) * (z // 2)
        return (z, near, 2 * (n - 1) - z - near - far, far)[i]

    tip = 2

    def cell(ref, i, a, which):
        return ref.at[i, which, pl.ds(kept * a, kept - tip if (i, a) == (n - 1, 0) else kept)]

    def end_cell(ref, which):
        return ref.at[n - 1, which, pl.ds(kept - tip, tip)]

    def end_copy():
        return remote(end_cell(mine, t), end_cell(theirs, t), end_send, end_recv, dp=1 - d)

    def far_copy(which):
        return remote(end_cell(mine, which), end_cell(theirs, which), far_send, far_recv, dp=1 - d, tm=1 - t)

    def sum_copy(i, a):
        return remote(
            cell(mine, i, a, t), cell(theirs, i, a, t), sum_send.at[3 * i + a], sum_recv.at[3 * i + a], dp=1 - d
        )

    def keep_copy(i, a, which):
        place = mine.at[i, which, pl.ds(kept * a, kept)]
        return remote(place, place, keep_send.at[3 * i + a], keep_recv.at[3 * i + a], tm=1 - t)

    def done_copy(i, a, which):
        place = cell(theirs, i, a, which)
        return remote(place, place, done_send.at[3 * i + a], done_recv.at[3 * i + a], tm=1 - t)

    def lane_of(shape):
        return lax.broadcasted_iota(jnp.int32, shape, len(shape) - 1)

    def matched(held, channels):
        cut = held.shape[0] // 32 * 16
        return jnp.concatenate(
            [
                lax.dot_general(x, channels, (((1,), (1,)), ((), ())), preferred_element_type=jnp.float32)
                for x in (held[:cut], held[cut:])
            ],
            axis=0,
        )

    def send_terms(i, a, terms):
        last = terms[kept * half :]
        for h in range(thirds):
            block = terms[h * extra * half : (h + 1) * extra * half]
            block = jnp.where(lane_of(block.shape) < c, block, pltpu.roll(last, c - spare * h, 1))
            mine[i, t, kept * a + h * extra : kept * a + (h + 1) * extra] = block.reshape(
                extra, half, lanes
            ).astype(jnp.bfloat16)
        mine[i, t, kept * a + thirds * extra : kept * (a + 1)] = terms[thirds * extra * half : kept * half].reshape(
            kept - thirds * extra, half, lanes
        ).astype(jnp.bfloat16)
        sum_copy(i, a).start()

    def kernel_terms(i):
        at = shard_rows(shard_of(i))

        def channels(first, count):
            return [
                act[at, first * pixels : (first + count) * pixels],
                jnp.zeros((spare, count * pixels), jnp.bfloat16),
            ]

        def held(first):
            return stack[:, half_rows(t), first * pixels : every * pixels].reshape(9 * half, (every - first) * pixels)

        pair = matched(held(0), jnp.concatenate(channels(1, every) + channels(2, every), axis=0))
        send_terms(i, 1, pair[:, :lanes])
        send_terms(i, 2, pair[:, lanes:])
        send_terms(i, 0, matched(held(2), jnp.concatenate(channels(2, every - 2), axis=0)))
        for a in range(3):
            keep_copy(i, a, t).start()
        if i == n - 1:
            end_copy().start()
            far_copy(t).start()

    def assemble(i, a, which):
        at = shard_of(i) * c
        both = (
            mine[i, which, kept * a : kept * (a + 1)].astype(jnp.float32)
            + theirs[i, which, kept * a : kept * (a + 1)].astype(jnp.float32)
        ) * scale
        last = None
        for h in reversed(range(thirds)):
            block = pltpu.roll(both[h * extra : (h + 1) * extra].reshape(extra * half, lanes), spare * (h + 1), 1)
            last = block if last is None else jnp.where(lane_of(block.shape) < spare * (h + 1), block, last)
        whole = jnp.concatenate([both.reshape(kept * half, lanes), last], axis=0)
        start = at % lanes
        turned_lanes = pltpu.roll(whole, start, 1).reshape(9, half, lanes)
        lane = lane_of(turned_lanes.shape)
        tile = at // lanes

        def put(tile, inside):
            place = (pl.ds(9 * a, 9), half_rows(which), pl.ds(pl.multiple_of(tile * lanes, lanes), lanes))
            kg_ref[place] = jnp.where(inside, turned_lanes, kg_ref[place])

        put(tile, (lane >= start) & (lane < start + c))

        @pl.when(start + c > lanes)
        def _():
            put(tile + 1, lane < start + c - lanes)

    def before(s):
        rhs = jnp.concatenate(
            [stack[:, :, frame_lanes(t * frames + s + 2 - a)].reshape(9 * c, pixels) for a in range(3)], axis=0
        )
        total = jnp.dot(turned[...], rhs, preferred_element_type=jnp.float32)
        for q in range(n):
            part[q, s] = total[q * c : (q + 1) * c].astype(jnp.bfloat16)

    few = frames // 2

    def share_right(q, h, src):
        at = pl.ds(h * few, few)
        return remote(src.at[q, at], right_in.at[q, at], right_send.at[2 * q + h], right_recv.at[2 * q + h], chan=z + 1)

    def share_left(q, h, src):
        at = pl.ds(h * few, few)
        return remote(src.at[q, at], left_in.at[q, at], left_send.at[2 * q + h], left_recv.at[2 * q + h], chan=z - 1)

    def first_share(j, h):
        @pl.when(z == 0)
        def _():
            share_right(n - 1 - j, h, part).start()

        @pl.when(z == n - 1)
        def _():
            share_left(j, h, part).start()

    def add_part(held, q, h):
        for s in range(h * few, (h + 1) * few):
            held[q, s] = (held[q, s].astype(jnp.float32) + part[q, s].astype(jnp.float32)).astype(jnp.bfloat16)

    def relay_right(q, h):
        share_right(q, h, right_in).wait_recv()
        add_part(right_in, q, h)
        share_right(q, h, right_in).start()

    def relay_left(q, h):
        share_left(q, h, left_in).wait_recv()
        add_part(left_in, q, h)
        share_left(q, h, left_in).start()

    def relay(k):
        kind, h = ((0, 0), (0, 1), (2, 0), (1, 0), (2, 1), (1, 1))[k]

        @pl.when(z == 1)
        def _():
            if kind == 2:
                relay_left(0, h)
            else:
                relay_right(n - 1 - kind, h)

        @pl.when(z == 2)
        def _():
            if kind == 2:
                relay_right(n - 1, h)
            else:
                relay_left(kind, h)

    def convolve(u):
        rhs = jnp.concatenate([act[:, frame_lanes(t * frames + u + a)] for a in range(3)], axis=0)
        lhs = jnp.concatenate([w_ref[9 * a : 9 * a + 9].reshape(9 * c, full) for a in range(3)], axis=1)
        taps[...] = jnp.dot(lhs, rhs, preferred_element_type=jnp.float32).reshape(9, c, pixels)
        result = jnp.zeros((c, pixels), jnp.float32)
        for i in range(3):
            for j in range(3):
                result = result + moved(taps[3 * i + j], i - 1, j - 1, pixels)
        frames_out[u] = result.astype(jnp.bfloat16)

    def forward(i):
        for a in (1, 2, 0):
            sum_copy(i, a).wait_recv()
            done_copy(i, a, t).start()
            assemble(i, a, t)

    def complete(i):
        for a in (1, 2, 0):
            keep_copy(i, a, 1 - t).wait_recv()
            done_copy(i, a, 1 - t).wait_recv()
            assemble(i, a, 1 - t)

    cot_copy().wait_recv()
    lax.fori_loop(0, frames, other_frame, 0)
    own_copy(1 - t).wait_recv()
    kernel_terms(0)

    @pl.when(t == 0)
    def _():
        halo_copy().wait_recv()

        def next_frame(s, _):
            stack_frame(cot_in[s, half_rows(1), :], frames + s, half_rows(1))
            return 0

        lax.fori_loop(0, 2, next_frame, 0)

    load_w.wait()
    turned[...] = jnp.transpose(w_ref[...].reshape(27 * c, full))
    before(0)
    before(1)
    first_share(0, 0)
    tick(0)
    before(2)
    before(3)
    first_share(0, 1)
    for j in range(1, n - 1):
        for h in range(2):
            first_share(j, h)
    tick(1)
    tick(2)
    for k in (0, 1, 2):
        pair_tick(k)
    kernel_terms(1)
    tick(3)
    tick(4)
    relay(0)
    tick(5)
    for k in (3, 4, 5):
        pair_tick(k)
    kernel_terms(2)
    relay(1)
    tick(6)
    forward(0)
    tick(7)
    relay(2)
    tick(8)
    for k in (6, 7, 8):
        pair_tick(k)
    kernel_terms(3)
    relay(3)
    relay(4)
    relay(5)
    complete(0)
    for u in range(frames):
        convolve(u)
    out_ref[...] = jnp.transpose(frames_out[...], (1, 0, 2))
    forward(1)
    complete(1)

    for h in range(2):
        @pl.when(z > 0)
        def _():
            share_right(z, h, right_in).wait_recv()

        @pl.when(z < n - 1)
        def _():
            share_left(z, h, left_in).wait_recv()

    def slope_frame(s, _):
        wide = f_ref[s].astype(jnp.float32)
        logistic = jax.nn.sigmoid(wide)
        slope = logistic * (1.0 + wide * (1.0 - logistic))

        def keep(total):
            frames_out[s] = (total * slope).astype(jnp.bfloat16)

        own = part[z, s].astype(jnp.float32)

        @pl.when(z == 0)
        def _():
            keep(own + left_in[z, s].astype(jnp.float32))

        @pl.when(z == n - 1)
        def _():
            keep(own + right_in[z, s].astype(jnp.float32))

        @pl.when((z > 0) & (z < n - 1))
        def _():
            keep(own + (left_in[z, s].astype(jnp.float32) + right_in[z, s].astype(jnp.float32)))

        return 0

    lax.fori_loop(0, frames, slope_frame, 0)
    fg_ref[...] = jnp.transpose(frames_out[...], (1, 0, 2))
    forward(2)
    complete(2)

    for p in range(total_pieces):
        @pl.when((z < n - 1) & (p < (z + 1) * per))
        def _():
            pass_right(p).wait_send()

        @pl.when((z > 0) & (p >= z * per))
        def _():
            pass_left(p).wait_send()

        @pl.when((p < z * per) | (p >= (z + 1) * per))
        def _():
            pair_copy(p, t).wait_send()

    for h in range(2):
        for j in range(n - 1):
            @pl.when(z < n - 1 - j)
            def _():
                share_right(n - 1 - j, h, right_in).wait_send()

            @pl.when(z > j)
            def _():
                share_left(j, h, left_in).wait_send()

    own_copy(t).wait_send()
    cot_copy().wait_send()

    @pl.when(t == 1)
    def _():
        halo_copy().wait_send()

    for i in range(n - 1):
        for a in range(3):
            sum_copy(i, a).wait_send()
            keep_copy(i, a, t).wait_send()
            done_copy(i, a, t).wait_send()

    for a in (1, 2):
        sum_copy(n - 1, a).wait_recv()
        done_copy(n - 1, a, t).start()
        assemble(n - 1, a, t)
    sum_copy(n - 1, 0).wait_recv()
    done_copy(n - 1, 0, t).start()
    for a in range(3):
        keep_copy(n - 1, a, 1 - t).wait_recv()
    for a in (1, 2):
        done_copy(n - 1, a, 1 - t).wait_recv()
        assemble(n - 1, a, 1 - t)
    end_copy().wait_recv()
    assemble(n - 1, 0, t)
    done_copy(n - 1, 0, 1 - t).wait_recv()
    far_copy(1 - t).wait_recv()
    assemble(n - 1, 0, 1 - t)
    end_copy().wait_send()
    far_copy(t).wait_send()
    for a in range(3):
        sum_copy(n - 1, a).wait_send()
        keep_copy(n - 1, a, t).wait_send()
        done_copy(n - 1, a, t).wait_send()


def write(out_ref, fg_ref, kg_ref, out_hbm, fg_hbm, kg_hbm, sems):
    copies = [
        pltpu.make_async_copy(kg_ref, kg_hbm, sems.at[0]),
        pltpu.make_async_copy(out_ref, out_hbm, sems.at[1]),
        pltpu.make_async_copy(fg_ref, fg_hbm, sems.at[2]),
    ]
    for copy in copies:
        copy.start()
    for copy in copies:
        copy.wait()


LANES = 128


def fits(mesh, features, kernel):
    c, clips, frames, pixels = features.shape
    return (
        mesh.shape["tm"] == 2
        and mesh.shape["chan"] == 4
        and mesh.shape["dp"] == 2
        and clips == 1
        and frames == 4
        and c * mesh.shape["chan"] == kernel.shape[2]
        and kernel.shape[2] == 3 * LANES
        and pixels % 128 == 0
        and pixels % WID == 0
        and kernel.size * 24 + features.size * 96 < 56 * 2**20
    )


def fused(mesh, features, kernel, cotangent):
    c, clips, frames, pixels = features.shape
    n = mesh.shape["chan"]
    full = c * n
    scale = 1.0 / math.sqrt(mesh.shape["dp"] * mesh.shape["tm"] * clips * frames * pixels)
    vmem = pl.BlockSpec(memory_space=pltpu.VMEM)
    hbm = pl.BlockSpec(memory_space=pltpu.HBM)
    b16, f32 = jnp.bfloat16, jnp.float32
    dma = pltpu.SemaphoreType.DMA
    half = c // 2
    rows = math.gcd(c, LANES)
    pieces = full // rows
    sums = 3 * n
    spare = LANES - c
    kept = 9 - 9 // (c // spare + 1)
    limit = 8 * 2**20 + kernel.size * 22 + features.size * 64
    in_hbm = lambda x: pltpu.with_memory_space_constraint(x, pltpu.HBM)
    shards = pltpu.VMEM((n, frames, c, pixels), b16)
    by_frame = pltpu.VMEM((frames, c, pixels), b16)
    by_channel = pltpu.VMEM((c, frames, pixels), b16)
    halves = pltpu.VMEM((n, 2, 3 * kept, half, LANES), b16)
    shapes = (
        jax.ShapeDtypeStruct((c, frames, pixels), b16),
        jax.ShapeDtypeStruct((c, frames, pixels), b16),
        jax.ShapeDtypeStruct((27, c, full), f32),
    )
    held = pl.pallas_call(
        functools.partial(body, (n, LANES, rows, scale)),
        out_shape=shapes,
        in_specs=[hbm, hbm, hbm],
        out_specs=(vmem,) * 3,
        scratch_shapes=[
            by_channel, by_channel, by_frame, by_frame,
            pltpu.VMEM((27, c, full), b16),
            pltpu.VMEM((9, c, (2 * frames + 2) * pixels), b16),
            pltpu.VMEM((full, 27 * c), b16),
            pltpu.VMEM((full, (2 * frames + 2) * pixels), b16),
            by_frame,
            shards, shards, shards,
            pltpu.VMEM((9, c, pixels), f32),
            by_frame,
            halves, halves,
            dma, dma, dma, dma((pieces,)), dma((pieces,)), dma((pieces,)), dma((pieces,)), dma((pieces,)), dma, dma,
            dma, dma, dma, dma, dma((2 * n,)), dma((2 * n,)), dma((2 * n,)), dma((2 * n,)),
            dma((sums,)), dma((sums,)), dma((sums,)), dma((sums,)), dma((sums,)), dma((sums,)), dma, dma, dma, dma,
        ],
        compiler_params=pltpu.CompilerParams(
            collective_id=0, has_side_effects=True, vmem_limit_bytes=limit
        ),
        name="video_conv",
    )(
        in_hbm(features.reshape(c, frames, pixels)),
        in_hbm(jnp.transpose(kernel, (1, 0, 2))),
        in_hbm(cotangent.reshape(c, frames, pixels)),
    )
    conv_out, feature_grad, kernel_grad = pl.pallas_call(
        write,
        out_shape=shapes,
        in_specs=[vmem] * 3,
        out_specs=(hbm,) * 3,
        scratch_shapes=[dma((3,))],
        compiler_params=pltpu.CompilerParams(vmem_limit_bytes=12 * 2**20),
        name="write",
    )(*held)
    return conv_out.reshape(features.shape), feature_grad.reshape(features.shape), jnp.transpose(kernel_grad, (1, 0, 2))


def solution(mesh):
    def chosen(features, kernel, cotangent):
        if fits(mesh, features, kernel):
            return fused(mesh, features, kernel, cotangent)
        return local(features, kernel, cotangent)

    return jax.shard_map(
        chosen,
        mesh=mesh,
        in_specs=(
            P("chan", ("groups", "dp"), "tm", None),
            P("chan", None, None),
            P("chan", ("groups", "dp"), "tm", None),
        ),
        out_specs=(
            P("chan", ("groups", "dp"), "tm", None),
            P("chan", ("groups", "dp"), "tm", None),
            P(("groups", "chan"), None, None),
        ),
        check_vma=False,
    )
```
